32 devices in a mesh: groups: 2 (over x), ctx: 16 (over z, y, core).
Axes of the slice: x: 2, y: 2, z: 4, core: 2. Of those that a mesh axis runs over, the one named last changes fastest.
Arguments:
- tokens: bfloat16 [16384, 1024], P(('groups', 'ctx')), parts along dimension 0
- w_qkv: bfloat16 [1024, 3072], P('ctx'), may hold values from -0.1875 to 0.1875
- w_out: bfloat16 [1024, 1024], P('ctx'), may hold values from -0.1875 to 0.1875
- var_bias: float32 [2, 16], replicated, may hold values from -2 to 2
- seg_id: int32 [16384], P(('groups', 'ctx')), parts along dimension 0, may hold values from 0 to 3, as said below
- var_id: int32 [16384], P(('groups', 'ctx')), parts along dimension 0, may hold values from 0 to 511
- time_id: int32 [16384], P(('groups', 'ctx')), parts along dimension 0, may hold values from 0 to 67
Outputs:
- mixed: bfloat16 [16384, 1024], P(('groups', 'ctx')), parts along dimension 0
The draws below stay inside these ranges and needn't reach their ends.
There are 2 independent parts, one for each index of `groups`. The reference program is written for one: setup_inputs(seed, part) draws one part's arguments, and reference() takes and returns one part's arrays. A program takes and returns all parts, laid end to end along the dimension named above; an argument that names none is the same for every part. Nothing has to cross between parts.
Inputs may be any that keep to these rules, and one draw needn't show every extreme that they name: seg_id starts at 0, never falls, and rises by at most one from a token to the next.
All inputs are finite; a program needn't handle non-finite values.
Results may differ from the reference program's by a relative error of at most 0.004.
The reference program's roundings to bfloat16 on the way (of `qkv`, `weight_bf` and `attended`) count: a program that leaves them out, or rounds other values in their place, can miss the bound.
Values may be sent and summed in bfloat16 or wider, within the bound.
No kernel may reach another device: no remote copies, remote signals or barrier semaphores. Data moves between devices by JAX's collectives and lax.ppermute only.
A program may use at most 256 MiB of HBM per device.

```python
import jax
import jax.numpy as jnp
from jax import lax

D = 1024
HEADS = 16
HEAD_DIM = 64
TOK_DEV = 512
TOKENS = 8192
REACH = 1023


def doc_layout(key):
    first_key, second_key = jax.random.split(jax.random.fold_in(key, 7))
    spans = TOKENS // (4 * TOK_DEV)
    span_index = jnp.arange(spans, dtype=jnp.int32)
    offsets = jax.random.randint(first_key, (spans,), 0, 2 * TOK_DEV)
    offsets = jnp.where(span_index == 0, 0, offsets)
    opening_pos = span_index * (4 * TOK_DEV) + offsets
    starts = jnp.zeros((TOKENS,), jnp.int32).at[opening_pos].set(1)
    places = jnp.arange(TOKENS, dtype=jnp.int32)
    segment = jnp.cumsum(starts) - 1
    opening = lax.cummax(jnp.where(starts == 1, places, 0))
    offset = places - opening
    table = jax.random.randint(second_key, (spans,), 4, 5 + TOK_DEV // 8)
    table = jnp.where(span_index == 0, 4, table)
    table = jnp.where(span_index == 1, 4 + TOK_DEV // 8, table)
    patches = table[segment]
    variate = jnp.minimum(offset // patches, TOK_DEV - 1)
    return (segment.astype(jnp.int32), variate.astype(jnp.int32), (offset % patches).astype(jnp.int32))


def draw_seg_id(key, part):
    return doc_layout(key)[0]


def draw_var_id(key, part):
    return doc_layout(key)[1]


def draw_time_id(key, part):
    return doc_layout(key)[2]


def draw_tokens(key, part):
    first_key = jax.random.fold_in(jax.random.fold_in(key, 11), 0)
    values = jnp.clip(jax.random.normal(first_key, (TOKENS, D), jnp.float32), -6.0, 6.0)
    return values.astype(jnp.bfloat16)


def shard_levels(stream_key, extent, pieces, least, high):
    def one(position, shards_of):
        steps = jax.random.uniform(jax.random.fold_in(jax.random.fold_in(stream_key, 6), position), (shards_of,), jnp.float32, least / len(pieces), high / len(pieces))
        return jnp.repeat(jnp.exp(steps), extent[position] // shards_of).reshape((-1,) + (1,) * (len(extent) - position - 1))

    loudness = one(*pieces[0])
    for cut in pieces[1:]:
        loudness = loudness * one(*cut)
    return loudness


def gaussian(key, extent, width, bound, cuts=(), held_as=jnp.bfloat16):
    array = jax.random.normal(key, extent, jnp.float32) * width
    if len(cuts) > 0:
        array = shard_levels(key, extent, cuts, -0.22, 0.18) * array
    return jnp.clip(array, min=-bound, max=bound).astype(held_as)


def setup_inputs(seed: int = 0, part: int = 0) -> dict:
    key_list = jax.random.split(jax.random.key(seed), 8)
    own_keys = jax.random.split(jax.random.fold_in(key_list[7], part), 8)
    tokens = draw_tokens(jax.random.fold_in(jax.random.fold_in(key_list[7], part), 71), part)
    w_qkv = gaussian(key_list[1], (D, 3 * D), D ** -0.5, 0.1875, ((0, 16),))
    w_out = gaussian(key_list[2], (D, D), D ** -0.5, 0.1875, ((0, 16),))
    var_bias = jnp.clip(jax.random.uniform(key_list[3], (2, HEADS), jnp.float32, -2.0, 2.0), -2.0, 2.0)
    seg_id = draw_seg_id(jax.random.fold_in(jax.random.fold_in(key_list[7], part), 71), part)
    var_id = draw_var_id(jax.random.fold_in(jax.random.fold_in(key_list[7], part), 71), part)
    time_id = draw_time_id(jax.random.fold_in(jax.random.fold_in(key_list[7], part), 71), part)
    return dict(tokens=tokens, w_qkv=w_qkv, w_out=w_out, var_bias=var_bias, seg_id=seg_id, var_id=var_id, time_id=time_id)


def reference(tokens, w_qkv, w_out, var_bias, seg_id, var_id, time_id):
    qkv = jnp.dot(tokens, w_qkv, preferred_element_type=jnp.float32).astype(jnp.bfloat16)
    qkv = lax.optimization_barrier(qkv).astype(jnp.float32)
    query = qkv[:, :D]
    keys = qkv[:, D:2 * D]
    values = qkv[:, 2 * D:]
    margin = 2 * TOK_DEV
    keys_pad = jnp.pad(keys, ((margin, margin), (0, 0)))
    values_pad = jnp.pad(values, ((margin, margin), (0, 0)))
    seg_pad = jnp.pad(seg_id, (margin, margin), constant_values=-1)
    var_pad = jnp.pad(var_id, (margin, margin))
    time_pad = jnp.pad(time_id, (margin, margin))
    scale = 1.0 / (HEAD_DIM ** 0.5)

    def block(index):
        start = (index * TOK_DEV).astype(jnp.int32)
        span = 5 * TOK_DEV
        q_blk = lax.dynamic_slice_in_dim(query, start, TOK_DEV, 0).reshape(TOK_DEV, HEADS, HEAD_DIM)
        k_blk = lax.dynamic_slice_in_dim(keys_pad, start, span, 0).reshape(span, HEADS, HEAD_DIM)
        v_blk = lax.dynamic_slice_in_dim(values_pad, start, span, 0).reshape(span, HEADS, HEAD_DIM)
        seg_q = lax.dynamic_slice_in_dim(seg_id, start, TOK_DEV, 0)
        var_q = lax.dynamic_slice_in_dim(var_id, start, TOK_DEV, 0)
        time_q = lax.dynamic_slice_in_dim(time_id, start, TOK_DEV, 0)
        seg_k = lax.dynamic_slice_in_dim(seg_pad, start, span, 0)
        var_k = lax.dynamic_slice_in_dim(var_pad, start, span, 0)
        time_k = lax.dynamic_slice_in_dim(time_pad, start, span, 0)
        q_pos = start + jnp.arange(TOK_DEV, dtype=jnp.int32)
        k_pos = start - margin + jnp.arange(span, dtype=jnp.int32)
        allowed = (seg_q[:, None] == seg_k[None, :]) & (time_k[None, :] <= time_q[:, None])
        allowed = allowed & (jnp.abs(q_pos[:, None] - k_pos[None, :]) <= REACH)
        same = var_q[:, None] == var_k[None, :]
        bias = jnp.where(same[None, :, :], var_bias[0][:, None, None], var_bias[1][:, None, None])
        score = jnp.einsum("qhe,khe->hqk", q_blk, k_blk) * scale + bias
        score = jnp.where(allowed[None, :, :], score, -1e30)
        peak = jnp.max(score, axis=-1, keepdims=True)
        weight = jnp.where(allowed[None, :, :], jnp.exp(score - peak), 0.0)
        total = jnp.sum(weight, axis=-1)
        weight_bf = lax.optimization_barrier(weight.astype(jnp.bfloat16)).astype(jnp.float32)
        summed = jnp.einsum("hqk,khe->qhe", weight_bf, v_blk)
        result = summed / jnp.transpose(total)[:, :, None]
        return result.reshape(TOK_DEV, D).astype(jnp.bfloat16)

    attended = lax.map(block, jnp.arange(TOKENS // TOK_DEV, dtype=jnp.int32)).reshape(TOKENS, D)
    return jnp.dot(attended, w_out, preferred_element_type=jnp.float32).astype(jnp.bfloat16)
```

```python
import functools
import math

import jax
import jax.numpy as jnp
from jax import lax
from jax.experimental import pallas as pl
from jax.experimental.pallas import tpu as pltpu
from jax.sharding import Mesh, PartitionSpec as P

BIG = 2.0**100
TIMES = 104
SEG_BITS = 8
TILE = 256
LOG2E = math.log2(math.e)
F32 = jnp.float32
BF16 = jnp.bfloat16


def project_kernel(hq, x0, x1, x2, x3, x4, x5, w_ref, k_ref, vt_ref, qt_ref):
    rows = x0.shape[0]
    for i, x in enumerate((x0, x1, x2, x3, x4, x5)):
        own = i in (1, 4)

        def body(j, carry, i=i, x=x, own=own):
            r = pl.multiple_of(j * TILE, TILE)
            xt = x[pl.ds(r, TILE), :]
            at = pl.multiple_of(i * rows + r, TILE)
            k_ref[pl.ds(at, TILE), :] = jnp.dot(xt, w_ref[:, hq : 2 * hq], preferred_element_type=F32).astype(BF16)
            v = lax.dot_general(xt, w_ref[:, 2 * hq :], (((1,), (0,)), ((), ())), preferred_element_type=F32)
            vt_ref[:, pl.ds(at, TILE)] = v.T.astype(BF16)
            if own:
                q = jnp.dot(xt, w_ref[:, :hq], preferred_element_type=F32).astype(BF16).astype(F32) * 0.125
                qt_ref[:, pl.ds(pl.multiple_of((0 if i == 1 else rows) + r, TILE), TILE)] = q.T.astype(BF16)
            return carry

        lax.fori_loop(0, rows // TILE, body, 0)


def attend_kernel(hsize, wide, tab_ref, delta_ref, k_ref, vt_ref, qt_ref, fk_ref, fqt_ref, vk_ref, vq_ref, o_ref, qa, sc):
    pair = pl.program_id(0)
    qi = pl.program_id(1)
    nt = sc.shape[0]
    zero = jnp.zeros((hsize, TILE), BF16)
    qa[0:hsize, 0:TILE] = qt_ref[0:hsize, :]
    qa[hsize : 2 * hsize, 0:TILE] = zero
    qa[0:hsize, TILE:] = zero
    qa[hsize : 2 * hsize, TILE:] = qt_ref[hsize : 2 * hsize, :]
    qa[2 * hsize :, 0:TILE] = fqt_ref[...]
    qa[2 * hsize :, TILE:] = fqt_ref[...]
    first = tab_ref[qi * wide]
    last = tab_ref[qi * wide + 1]
    da = delta_ref[2 * pair]
    db = delta_ref[2 * pair + 1]

    def place(kk):
        return pl.multiple_of(tab_ref[qi * wide + 2 + kk], TILE)

    def scores(kk, edge):
        at = place(kk)
        lhs = jnp.concatenate([k_ref[pl.ds(at, TILE), :], fk_ref[pl.ds(at, TILE), :]], axis=1)
        s = jnp.dot(lhs, qa[...], preferred_element_type=F32)
        if edge:
            r = lax.broadcasted_iota(jnp.int32, (TILE, TILE), 0)
            p = lax.broadcasted_iota(jnp.int32, (TILE, TILE), 1)
            ok = (r > p) if edge < 0 else (r < p)
            ok = jnp.concatenate([ok, ok], axis=1)
            s = jnp.where(ok, s, -BIG)
        sc[kk] = s

        @pl.when(tab_ref[qi * wide + 2 + nt + kk] != 0)
        def _():
            vk = vk_ref[pl.ds(at, TILE), :]
            same = jnp.concatenate([vk, vk], axis=1) == vq_ref[...]
            sc[kk, :, 0:TILE] += jnp.where(same, da, 0.0)
            sc[kk, :, TILE:] += jnp.where(same, db, 0.0)

    @pl.when(first == 0)
    def _():
        scores(0, -1)

    @pl.when(last == nt)
    def _():
        scores(nt - 1, 1)

    def inner(kk, carry):
        scores(kk, 0)
        return carry

    lax.fori_loop(jnp.maximum(first, 1), jnp.minimum(last, nt - 1), inner, 0)

    def peak(kk, m):
        return jnp.maximum(m, jnp.max(sc[kk].reshape(TILE // 8, 8, 2 * TILE), axis=0))

    m = lax.fori_loop(first, last, peak, jnp.full((8, 2 * TILE), -BIG, F32))
    m = jnp.max(m, axis=0, keepdims=True)

    def mix(kk, carry):
        tot, oa, ob = carry
        w = jnp.exp2((sc[kk] - m) * LOG2E)
        tot = tot + jnp.sum(w.reshape(TILE // 8, 8, 2 * TILE), axis=0)
        wb = w.astype(BF16)
        vt = vt_ref[:, pl.ds(place(kk), TILE)]
        oa = oa + jnp.dot(vt[0:hsize], wb[:, 0:TILE], preferred_element_type=F32)
        ob = ob + jnp.dot(vt[hsize:], wb[:, TILE:], preferred_element_type=F32)
        return tot, oa, ob

    z = jnp.zeros((hsize, TILE), F32)
    tot, oa, ob = lax.fori_loop(first, last, mix, (jnp.zeros((8, 2 * TILE), F32), z, z))
    tot = jnp.sum(tot, axis=0, keepdims=True)
    o_ref[0:hsize, :] = (oa / tot[:, 0:TILE]).astype(BF16)
    o_ref[hsize:, :] = (ob / tot[:, TILE:]).astype(BF16)


def local(chips, tokens, w_qkv, w_out, var_bias, seg_id, var_id, time_id):
    rows, width = tokens.shape
    heads = var_bias.shape[1]
    hsize = width // heads
    hq = width // 2
    core = lax.axis_index("core")
    chip = lax.axis_index("chip")
    swap = [(0, 1), (1, 0)]
    up = [(i, i + 1) for i in range(chips - 1)]
    down = [(i + 1, i) for i in range(chips - 1)]

    def half(w, c):
        return jnp.concatenate([lax.dynamic_slice_in_dim(w, a * width + c * hq, hq, 1) for a in range(3)], 1)

    got = lax.ppermute(half(w_qkv, 1 - core), "core", swap)
    mine = half(w_qkv, core)
    both = jnp.where(core == 0, jnp.concatenate([mine, got], 0), jnp.concatenate([got, mine], 0))
    w = lax.all_gather(both, "chip", axis=0, tiled=True)
    w_o = lax.all_gather(w_out, ("chip", "core"), axis=0, tiled=True)

    def spread(a):
        before = lax.ppermute(a, "chip", up)
        after = lax.ppermute(a, "chip", down)
        return [before, a, after] + [lax.ppermute(t, "core", swap) for t in (before, a, after)]

    ids = jnp.stack([seg_id, var_id, time_id], 0)
    xs = spread(tokens)
    seg, var, time = jnp.concatenate(spread(ids), 1)

    nk = 6 * rows
    per = rows // TILE
    nt = 2 * ((2 * rows) // TILE) + 1
    nq = 2 * per
    there = jnp.stack([chip > 0, chip >= 0, chip < chips - 1]).astype(jnp.int32)
    there = jnp.repeat(jnp.tile(there, 2), rows)
    bits = jnp.arange(SEG_BITS, dtype=jnp.int32)
    seg_bit = ((seg[:, None] >> bits[None, :]) & 1).astype(F32)
    late = (time[:, None] > jnp.arange(TIMES, dtype=jnp.int32)[None, :]).astype(F32)
    pad = jnp.zeros((nk, 128 - TIMES - 2 * SEG_BITS - 1), F32)
    fk = -BIG * jnp.concatenate([late, seg_bit, 1.0 - seg_bit, 1.0 - there.astype(F32)[:, None], pad], 1)
    fk = fk.astype(BF16)

    def mine_of(a):
        return jnp.concatenate([a[rows : 2 * rows], a[4 * rows : 5 * rows]], 0)

    seg_q, var_q, time_q = mine_of(seg), mine_of(var), mine_of(time)
    qbit = ((seg_q[None, :] >> bits[:, None]) & 1).astype(F32)
    at_time = (time_q[None, :] == jnp.arange(TIMES, dtype=jnp.int32)[:, None]).astype(F32)
    fqt = jnp.concatenate([at_time, 1.0 - qbit, qbit, jnp.ones((1, 2 * rows), F32), jnp.zeros((128 - TIMES - 2 * SEG_BITS - 1, 2 * rows), F32)], 0)
    fqt = fqt.astype(BF16)

    qtile = jnp.arange(nq, dtype=jnp.int32)
    q_core = jnp.where(qtile // per == 0, core, 1 - core)
    q_win = (2 + q_core) * per + qtile % per
    k_win = q_win[:, None] - 2 * per + jnp.arange(nt, dtype=jnp.int32)[None, :]
    kblock = k_win // per
    kplace = (jnp.where(kblock % 2 == core, 0, 3) + kblock // 2) * per + k_win % per
    code = seg * 1024 + var
    tiles = code.reshape(nk // TILE, TILE)
    lo, hi = tiles.min(1), tiles.max(1)
    slo, shi = lo // 1024, hi // 1024
    ok = there.reshape(nk // TILE, TILE)[:, 0]
    qlo, qhi = mine_of_tiles(lo, per), mine_of_tiles(hi, per)
    use = (ok[kplace] > 0) & (slo[kplace] <= (qhi // 1024)[:, None]) & (shi[kplace] >= (qlo // 1024)[:, None])
    share = (lo[kplace] <= qhi[:, None]) & (hi[kplace] >= qlo[:, None])
    index = jnp.arange(nt, dtype=jnp.int32)[None, :]
    first = jnp.min(jnp.where(use, index, nt), 1)
    last = jnp.max(jnp.where(use, index + 1, 0), 1)
    wide = 2 + 2 * nt
    table = jnp.concatenate([first[:, None], last[:, None], kplace * TILE, share.astype(jnp.int32)], 1).reshape(-1)
    delta = lax.dynamic_slice_in_dim(var_bias[0] - var_bias[1], core * (heads // 2), heads // 2, 0)
    vk = jnp.broadcast_to(var[:, None], (nk, 128))

    vm = pl.BlockSpec(memory_space=pltpu.VMEM)
    k, vt, qt = pl.pallas_call(
        functools.partial(project_kernel, hq),
        out_shape=[
            jax.ShapeDtypeStruct((nk, hq), BF16),
            jax.ShapeDtypeStruct((hq, nk), BF16),
            jax.ShapeDtypeStruct((hq, 2 * rows), BF16),
        ],
        in_specs=[vm] * 7,
        out_specs=[vm] * 3,
        compiler_params=pltpu.CompilerParams(vmem_limit_bytes=48 << 20),
        name="project",
    )(*xs, w)

    att = pl.pallas_call(
        functools.partial(attend_kernel, hsize, wide),
        out_shape=jax.ShapeDtypeStruct((hq, 2 * rows), BF16),
        grid_spec=pltpu.PrefetchScalarGridSpec(
            num_scalar_prefetch=2,
            grid=(heads // 4, nq),
            in_specs=[
                pl.BlockSpec((nk, 2 * hsize), lambda p, q, *_: (0, p)),
                pl.BlockSpec((2 * hsize, nk), lambda p, q, *_: (p, 0)),
                pl.BlockSpec((2 * hsize, TILE), lambda p, q, *_: (p, q)),
                pl.BlockSpec((nk, 128), lambda p, q, *_: (0, 0)),
                pl.BlockSpec((128, TILE), lambda p, q, *_: (0, q)),
                pl.BlockSpec((nk, 128), lambda p, q, *_: (0, 0)),
                pl.BlockSpec((1, TILE), lambda p, q, *_: (0, q)),
            ],
            out_specs=pl.BlockSpec((2 * hsize, TILE), lambda p, q, *_: (p, q)),
            scratch_shapes=[
                pltpu.VMEM((2 * hsize + 128, 2 * TILE), BF16),
                pltpu.VMEM((nt, TILE, 2 * TILE), F32),
            ],
        ),
        compiler_params=pltpu.CompilerParams(vmem_limit_bytes=48 << 20),
        name="attend",
    )(table, delta, k, vt, qt, fk, fqt, vk, var_q[None, :])

    mine_att = att[:, :rows]
    got_att = lax.ppermute(att[:, rows:], "core", swap)
    w_mine = lax.dynamic_slice_in_dim(w_o, core * hq, hq, 0)
    w_got = lax.dynamic_slice_in_dim(w_o, (1 - core) * hq, hq, 0)

    def down_dot(a, b):
        return lax.dot_general(a, b, (((0,), (0,)), ((), ())), preferred_element_type=F32)

    return (down_dot(mine_att, w_mine) + down_dot(got_att, w_got)).astype(BF16)


def mine_of_tiles(a, per):
    return jnp.concatenate([a[per : 2 * per], a[4 * per : 5 * per]], 0)


def solution(mesh):
    groups, ctx = mesh.shape["groups"], mesh.shape["ctx"]
    chips = ctx // 2
    mesh3 = Mesh(mesh.devices.reshape(groups, chips, 2), ("groups", "chip", "core"))
    toks = ("groups", "chip", "core")
    par = ("chip", "core")
    in_specs = (P(toks, None), P(par, None), P(par, None), P(), P(toks), P(toks), P(toks))
    return jax.shard_map(
        functools.partial(local, chips), mesh=mesh3, in_specs=in_specs, out_specs=P(toks, None), check_vma=False
    )
```

```python
import functools
import math

import jax
import jax.numpy as jnp
from jax import lax
from jax.experimental import pallas as pl
from jax.experimental.pallas import tpu as pltpu
from jax.sharding import Mesh, PartitionSpec as P

BIG = 2.0**100
TIMES = 104
SEG_BITS = 8
TILE = 256
CHUNKS = 2
LOG2E = math.log2(math.e)
F32 = jnp.float32
BF16 = jnp.bfloat16
I32 = jnp.int32


def pick_kernel(width, cols, wide, pairs, who_ref, w_ref, *outs):
    me, half = who_ref[0], who_ref[1]
    for step, out in enumerate(outs):
        to = me ^ step
        for a in range(3):
            for b in range(pairs):
                at = pl.multiple_of(a * width + to * cols + (half ^ b if pairs == 1 else b) * wide, wide)
                out[:, (a * pairs + b) * wide : (a * pairs + b + 1) * wide] = w_ref[:, pl.ds(at, wide)]


def project_kernel(cols, plan, queries, planes, couple, who_ref, *refs):
    n = len(plan)
    k_ref, vt_ref, qt_ref, w = refs[-4:]
    xs, parts = refs[:n], refs[n:-4]
    me, plane, half = who_ref[0], who_ref[1], who_ref[2]
    wide = cols // 2
    rows = w.shape[0] // (4 * planes)
    for i, part in enumerate(parts):
        pair = half if i == 0 else 1 - half
        for p in range(planes):
            source = lax.rem(plane + planes - p, planes)
            for step in range(4):
                to = pl.multiple_of((4 * source + (me ^ step)) * rows, rows)
                block = part[(4 * p + step) * rows : (4 * p + step + 1) * rows, :]
                if couple:
                    for a in range(3):
                        at = pl.multiple_of(a * cols + pair * wide, wide)
                        w[pl.ds(to, rows), pl.ds(at, wide)] = block[:, a * wide : (a + 1) * wide]
                else:
                    w[pl.ds(to, rows), :] = block
    for x, at in zip(xs, plan):
        rows = x.shape[0]
        out = jnp.dot(x[...], w[...], preferred_element_type=F32)
        k_ref[at : at + rows, :] = out[:, cols : 2 * cols].astype(BF16)
        vt_ref[:, at : at + rows] = out[:, 2 * cols :].astype(BF16).T
        if at in queries:
            q = (out[:, :cols].astype(BF16) * 0.125).astype(BF16)
            qt_ref[:, queries[at] : queries[at] + rows] = q.T


def attend_kernel(
    hsize, q0, nq, tab_ref, delta_ref, k_ref, vt_ref, qt_ref, fk_ref, fqt_ref, vk_ref, vq_ref, o_ref, qa0, qa1, sc0, sc1, m0, m1
):
    qi = pl.program_id(0)
    qas, scs, ms = (qa0, qa1), (sc0, sc1), (m0, m1)
    nt = sc0.shape[0]
    wide = nt + 1
    two = 2 * hsize

    def place(q, kk):
        return pl.multiple_of(tab_ref[(q0 + q) * wide + kk], TILE)

    def lanes(q):
        return pl.ds(pl.multiple_of((q0 + q) * TILE, TILE), TILE)

    def prep():
        zero = jnp.zeros((hsize, TILE), BF16)
        for j, qa in enumerate(qas):
            qa[0:hsize, 0:TILE] = qt_ref[two * j : two * j + hsize, lanes(qi)]
            qa[0:hsize, TILE:] = zero
            qa[hsize:two, 0:TILE] = zero
            qa[hsize:two, TILE:] = qt_ref[two * j + hsize : two * (j + 1), lanes(qi)]
            f = fqt_ref[:, lanes(qi)]
            qa[two:, 0:TILE] = f
            qa[two:, TILE:] = f

    def scores(j, kk, share, m):
        at = place(qi, kk)
        lhs = jnp.concatenate([k_ref[pl.ds(at, TILE), two * j : two * (j + 1)], fk_ref[pl.ds(at, TILE), :]], axis=1)
        s = jnp.dot(lhs, qas[j][...], preferred_element_type=F32)
        if kk in (0, nt - 1):
            r = lax.broadcasted_iota(I32, (TILE, TILE), 0)
            p = lax.broadcasted_iota(I32, (TILE, TILE), 1)
            ok = (r > p) if kk == 0 else (r < p)
            s = jnp.where(jnp.concatenate([ok, ok], axis=1), s, -BIG)
        if share:
            vk = vk_ref[pl.ds(at, TILE), :]
            same = jnp.concatenate([vk, vk], axis=1) == vq_ref[:, lanes(qi)]
            s = s + jnp.concatenate(
                [jnp.where(same, delta_ref[2 * j], 0.0), jnp.where(same, delta_ref[2 * j + 1], 0.0)], axis=1
            )
        scs[j][kk] = s
        return jnp.maximum(m, jnp.max(s.reshape(TILE // 8, 8, 2 * TILE), axis=0))

    def mix(j, q, kk, top, state):
        tot, oa, ob = state
        vt = vt_ref[two * j : two * (j + 1), pl.ds(place(q, kk), TILE)]
        w = jnp.exp2((scs[j][kk] - top) * LOG2E)
        tot = tot + jnp.sum(w.reshape(TILE // 8, 8, 2 * TILE), axis=0)
        wb = w.astype(BF16)
        oa = oa + jnp.dot(vt[:hsize], wb[:, :TILE], preferred_element_type=F32)
        ob = ob + jnp.dot(vt[hsize:], wb[:, TILE:], preferred_element_type=F32)
        return tot, oa, ob

    def phase(j, old, q, share):
        m = jnp.full((8, 2 * TILE), -BIG, F32)
        z = jnp.zeros((hsize, TILE), F32)
        state = (jnp.zeros((8, 2 * TILE), F32), z, z)
        if old is not None:
            top = jnp.max(ms[old][...], axis=0, keepdims=True)
        for kk in range(nt):
            if j is not None:
                m = scores(j, kk, share or abs(kk - nt // 2) <= 1, m)
            if old is not None:
                state = mix(old, q, kk, top, state)
        if j is not None:
            ms[j][...] = m
        if old is not None:
            tot, oa, ob = state
            tot = jnp.sum(tot, axis=0, keepdims=True)
            o = jnp.concatenate([oa / tot[:, :TILE], ob / tot[:, TILE:]], axis=0)
            o_ref[pl.ds(pl.multiple_of(q * TILE, TILE), TILE), two * old : two * (old + 1)] = o.T.astype(BF16)

    prep()
    far = tab_ref[(q0 + qi) * wide + nt]
    for share in (False, True):

        @pl.when((far != 0) == share)
        def _(share=share):
            @pl.when(qi == 0)
            def _():
                phase(0, None, 0, share)

            @pl.when(qi > 0)
            def _():
                phase(0, 1, qi - 1, share)

            phase(1, 0, qi, share)

    @pl.when(qi == nq - 1)
    def _():
        phase(None, 1, qi, False)


def out_kernel(planes, who_ref, a0, a1, a2, a3, w0, w1, w2, o_ref, w):
    me, plane = who_ref[0], who_ref[1]
    for part, place in ((w0, me), (w1.at[0], me ^ 1), (w2, me ^ 2), (w1.at[1], me ^ 3)):
        rows = part.shape[0] // planes
        for i in range(planes):
            source = lax.rem(plane + planes - i, planes)
            at = pl.multiple_of((4 * source + place) * rows, rows)
            w[pl.ds(at, rows), :] = part[i * rows : (i + 1) * rows, :]
    total = None
    for a, place in ((a0, me), (a1, me ^ 1), (a2, me ^ 2), (a3, me ^ 3)):
        cols = a.shape[1]
        part = jnp.dot(a[...], w[pl.ds(pl.multiple_of(place * cols, cols), cols), :], preferred_element_type=F32)
        total = part if total is None else total + part
    o_ref[...] = total.astype(BF16)


def in_plane(blocks):
    swap = [(0, 1), (1, 0)]
    cross = [(0, 3), (1, 2), (2, 1), (3, 0)]
    return [
        lax.ppermute(blocks[0], "core", swap),
        lax.ppermute(blocks[1], "side", swap),
        lax.ppermute(blocks[2], ("side", "core"), cross),
    ]


def work(micros):
    return pl.CostEstimate(flops=int(micros * 1.1e9), transcendentals=0, bytes_accessed=1 << 20)


def turns(block, planes):
    return [block] + [
        lax.ppermute(block, "plane", [(i, (i + s) % planes) for i in range(planes)]) for s in range(1, planes)
    ]


def local(groups, planes, tokens, w_qkv, w_out, var_bias, seg_id, var_id, time_id):
    rows, width = tokens.shape
    heads = var_bias.shape[1]
    hsize = width // heads
    cols = width // 4
    core = lax.axis_index("core")
    side = lax.axis_index("side")
    plane = lax.axis_index("plane")
    swap = [(0, 1), (1, 0)]
    cross = [(0, 3), (1, 2), (2, 1), (3, 0)]
    pair = ("plane", "side")
    native, passed, direct = [], [], []
    for p in range(planes - 1):
        native += [(2 * (p + 1), 2 * p), (2 * p + 1, 2 * (p + 1) + 1)]
        passed += [(2 * p, 2 * (p + 1)), (2 * (p + 1) + 1, 2 * p + 1)]
        direct += [(2 * p + 1, 2 * (p + 1)), (2 * (p + 1), 2 * p + 1)]

    group = lax.axis_index("groups")
    me = 2 * side + core
    wide = cols // 2
    mate = [(g, g ^ 1) for g in range(groups)]
    couple = groups % 2 == 0
    picked = pl.pallas_call(
        functools.partial(pick_kernel, width, cols, wide, 1 if couple else 2),
        out_shape=[jax.ShapeDtypeStruct((w_qkv.shape[0], (3 if couple else 6) * wide), BF16)] * 4,
        in_specs=[pl.BlockSpec(memory_space=pltpu.SMEM), pl.BlockSpec(memory_space=pltpu.VMEM)],
        out_specs=[pl.BlockSpec(memory_space=pltpu.VMEM)] * 4,
        cost_estimate=work(1),
        name="pick",
    )(jnp.stack([me, group % 2]).astype(I32), w_qkv)
    came = in_plane(picked[1:])
    plane_w = jnp.concatenate([picked[0]] + came, 0)
    w_parts = turns(plane_w, planes)
    turned = w_parts[1:]
    if couple:
        half_w = jnp.concatenate(w_parts, 0)
        w_parts = [half_w, lax.ppermute(half_w, "groups", mate)]
    else:
        w_parts = [jnp.concatenate(w_parts, 0)]

    ids = jnp.stack([seg_id, var_id, time_id], 0)
    ids = [ids] + [lax.ppermute(ids, a, to) for a, to in (("side", swap), (pair, native), (pair, direct))]
    tokens_y = lax.optimization_barrier((tokens, came, ids))[0]
    tokens_z = lax.optimization_barrier((tokens, turned))[0]
    ids = jnp.concatenate(ids, 1)
    ids = jnp.concatenate([ids, lax.ppermute(ids, "core", swap)], 1)

    cut = rows // CHUNKS
    pieces = [tokens_y[c * cut : (c + 1) * cut] for c in range(CHUNKS)]
    other = [lax.ppermute(x, "side", swap) for x in pieces]
    mine = lax.ppermute(tokens_z, pair, native)
    theirs = [lax.ppermute(x, pair, passed) for x in other]
    xs = [(0, tokens)] + [(rows + c * cut, x) for c, x in enumerate(other)]
    xs = xs + [(2 * rows, mine)] + [(3 * rows + c * cut, x) for c, x in enumerate(theirs)]
    tokens_c = lax.optimization_barrier((tokens, other))[0]
    xs = xs + [(4 * rows + at, lax.ppermute(x if at else tokens_c, "core", swap)) for at, x in xs]
    plan = tuple(at for at, _ in xs)
    xs = [x for _, x in xs]

    nk = 8 * rows
    per = rows // TILE
    nt = 4 * per + 1
    nq = 2 * per
    seg, var, time = ids
    below = jnp.where(side == 0, 3, 2)
    stream = jnp.arange(4, dtype=I32)
    there = jnp.where(stream == below, plane > 0, jnp.where(stream == 5 - below, plane < planes - 1, True))
    there = jnp.tile(there, 2)
    gone = jnp.repeat(~there, rows)
    col = lax.broadcasted_iota(I32, (1, 128), 1)
    bit0, bit1, last = TIMES, TIMES + SEG_BITS, TIMES + 2 * SEG_BITS
    one = (seg[:, None] >> jnp.clip(col - bit0, 0, 30)) & 1
    zero = 1 - ((seg[:, None] >> jnp.clip(col - bit1, 0, 30)) & 1)
    off = jnp.where(
        col < bit0,
        time[:, None] > col,
        jnp.where(col < bit1, one == 1, jnp.where(col < last, zero == 1, (col == last) & gone[:, None])),
    )
    fk = jnp.where(off, -BIG, 0.0).astype(BF16)

    def asked(a):
        return jnp.concatenate([a[0:rows], a[4 * rows : 5 * rows], a[rows : 2 * rows], a[5 * rows : 6 * rows]], 0)

    seg_q, var_q, time_q = asked(seg)[None, :], asked(var)[None, :], asked(time)[None, :]
    row = lax.broadcasted_iota(I32, (128, 1), 0)
    qone = ((seg_q >> jnp.clip(row - bit1, 0, 30)) & 1) == 1
    qzero = ((seg_q >> jnp.clip(row - bit0, 0, 30)) & 1) == 0
    on = jnp.where(row < bit0, time_q == row, jnp.where(row < bit1, qzero, jnp.where(row < last, qone, row == last)))
    fqt = jnp.where(on, 1.0, 0.0).astype(BF16)
    vk = jnp.broadcast_to(var[:, None], (nk, 128))

    qtile = jnp.arange(4 * per, dtype=I32)
    qblock = qtile // per
    q_side = jnp.where(qblock // 2 == 0, side, 1 - side)
    q_core = jnp.where(qblock % 2 == 0, core, 1 - core)
    q_win = (2 + 2 * q_side + q_core) * per + qtile % per
    k_win = q_win[:, None] - 2 * per + jnp.arange(nt, dtype=I32)[None, :]
    k_block = k_win // per
    k_token = k_block // 2
    k_stream = jnp.where(
        side == 0,
        jnp.where(k_token == 0, 3, k_token - 1),
        jnp.where(k_token == 3, 3, 2 - k_token),
    )
    k_place = (jnp.where(k_block % 2 == core, 0, 4) + k_stream) * per + k_win % per
    code = (seg * 1024 + var).reshape(nk // TILE, TILE)
    lo, hi = code.min(1), code.max(1)
    ask = jnp.concatenate([jnp.arange(per, dtype=I32) + b * per for b in (0, 4, 1, 5)])
    share = (lo[k_place] <= hi[ask][:, None]) & (hi[k_place] >= lo[ask][:, None])
    share = share & jnp.repeat(there, per)[k_place]
    share = share & (jnp.abs(jnp.arange(nt, dtype=I32) - nt // 2) > 1)[None, :]
    table = jnp.concatenate([k_place * TILE, share.any(1, keepdims=True).astype(I32)], 1).reshape(-1)
    delta = lax.dynamic_slice_in_dim(var_bias[0] - var_bias[1], (2 * side + core) * (heads // 4), heads // 4, 0)

    vm = pl.BlockSpec(memory_space=pltpu.VMEM)
    limit = pltpu.CompilerParams(vmem_limit_bytes=48 << 20)
    queries = {}
    for at, x in zip(plan, xs):
        block = at // rows
        if block in (0, 1, 4, 5):
            queries[at] = {0: 0, 4: rows, 1: 2 * rows, 5: 3 * rows}[block] + at % rows
    k, vt, qt = pl.pallas_call(
        functools.partial(project_kernel, cols, plan, queries, planes, couple),
        out_shape=[
            jax.ShapeDtypeStruct((nk, cols), BF16),
            jax.ShapeDtypeStruct((cols, nk), BF16),
            jax.ShapeDtypeStruct((cols, 4 * rows), BF16),
        ],
        in_specs=[pl.BlockSpec(memory_space=pltpu.SMEM)] + [vm] * (len(xs) + len(w_parts)),
        out_specs=[vm] * 3,
        scratch_shapes=[pltpu.VMEM((width, 3 * cols), BF16)],
        compiler_params=limit,
        cost_estimate=work(12),
        name="project",
    )(jnp.stack([me, plane, group % 2]).astype(I32), *xs, *w_parts)

    late_w, qt = lax.optimization_barrier((w_out, qt))
    wo = jnp.concatenate(turns(late_w, planes), 0)
    wo_side = lax.ppermute(wo, "side", swap)
    wo_core = lax.ppermute(jnp.stack([wo, wo_side]), "core", swap)
    wo_parts = [wo, wo_core, wo_side]

    def attend(q0):
        return pl.pallas_call(
            functools.partial(attend_kernel, hsize, q0, nq),
            out_shape=jax.ShapeDtypeStruct((2 * rows, cols), BF16),
            grid_spec=pltpu.PrefetchScalarGridSpec(
                num_scalar_prefetch=2,
                grid=(nq,),
                in_specs=[vm] * 7,
                out_specs=vm,
                scratch_shapes=[pltpu.VMEM((2 * hsize + 128, 2 * TILE), BF16)] * 2
                + [pltpu.VMEM((nt, TILE, 2 * TILE), F32)] * 2
                + [pltpu.VMEM((8, 2 * TILE), F32)] * 2,
            ),
            compiler_params=limit,
            cost_estimate=work(16),
            name="attend",
        )(table, delta, k, vt, qt, fk, fqt, vk, var_q)

    far = attend(nq)
    far_side = lax.ppermute(far[:rows], "side", swap)
    far_cross = lax.ppermute(far[rows:], ("side", "core"), cross)
    near = attend(0)
    near_core = lax.ppermute(near[rows:], "core", swap)
    return pl.pallas_call(
        functools.partial(out_kernel, planes),
        out_shape=jax.ShapeDtypeStruct((rows, width), BF16),
        in_specs=[pl.BlockSpec(memory_space=pltpu.SMEM)] + [vm] * 7,
        out_specs=vm,
        scratch_shapes=[pltpu.VMEM((width, width), BF16)],
        compiler_params=limit,
        cost_estimate=work(3),
        name="mixed",
    )(jnp.stack([me, plane]).astype(I32), near[:rows], near_core, far_side, far_cross, *wo_parts)


def solution(mesh):
    groups, ctx = mesh.shape["groups"], mesh.shape["ctx"]
    planes = ctx // 4
    mesh4 = Mesh(mesh.devices.reshape(groups, planes, 2, 2), ("groups", "plane", "side", "core"))
    toks = ("groups", "plane", "side", "core")
    par = ("plane", "side", "core")
    in_specs = (P(toks, None), P(par, None), P(par, None), P(), P(toks), P(toks), P(toks))
    return jax.shard_map(
        functools.partial(local, groups, planes), mesh=mesh4, in_specs=in_specs, out_specs=P(toks, None), check_vma=False
    )
```

```python
import functools
import math

import jax
import jax.numpy as jnp
from jax import lax
from jax.experimental import pallas as pl
from jax.experimental.pallas import tpu as pltpu
from jax.sharding import Mesh, PartitionSpec as P

BIG = 2.0**100
TIMES = 104
SEG_BITS = 8
TILE = 256
ID_ROWS = 16
LOG2E = math.log2(math.e)
F32 = jnp.float32
BF16 = jnp.bfloat16
I32 = jnp.int32


def pick_kernel(width, cols, wide, pairs, who_ref, w_ref, *outs):
    me, half = who_ref[0], who_ref[1]
    for step, out in enumerate(outs):
        to = me ^ step
        for a in range(3):
            for b in range(pairs):
                at = pl.multiple_of(a * width + to * cols + (half ^ b if pairs == 1 else b) * wide, wide)
                out[:, (a * pairs + b) * wide : (a * pairs + b + 1) * wide] = w_ref[:, pl.ds(at, wide)]


def project_kernel(cols, plan, queries, planes, couple, who_ref, *refs):
    n = len(plan)
    k_ref, vt_ref, qt_ref, w = refs[-4:]
    xs, parts = refs[:n], refs[n:-4]
    me, plane, half = who_ref[0], who_ref[1], who_ref[2]
    wide = cols // 2
    rows = w.shape[0] // (4 * planes)
    for i, part in enumerate(parts):
        pair = half if i == 0 else 1 - half
        for p in range(planes):
            source = lax.rem(plane + planes - p, planes)
            for step in range(4):
                to = pl.multiple_of((4 * source + (me ^ step)) * rows, rows)
                block = part[(4 * p + step) * rows : (4 * p + step + 1) * rows, :]
                if couple:
                    for a in range(3):
                        at = pl.multiple_of(a * cols + pair * wide, wide)
                        w[pl.ds(to, rows), pl.ds(at, wide)] = block[:, a * wide : (a + 1) * wide]
                else:
                    w[pl.ds(to, rows), :] = block
    for x, (at, rows) in zip(xs, plan):
        out = jnp.dot(x[0:rows, :], w[:, cols:], preferred_element_type=F32)
        k_ref[at : at + rows, :] = out[:, :cols].astype(BF16)
        vt_ref[:, at : at + rows] = out[:, cols:].astype(BF16).T
        if at in queries:
            out = jnp.dot(x[0:rows, :], w[:, :cols], preferred_element_type=F32)
            q = (out.astype(BF16) * 0.125).astype(BF16)
            qt_ref[:, queries[at] : queries[at] + rows] = q.T


def mask_kernel(keys_ref, asks_ref, fk_ref, vk_ref, fqt_ref):
    bit0, bit1, last = TIMES, TIMES + SEG_BITS, TIMES + 2 * SEG_BITS

    def bit(seg, row, start):
        return (seg >> jnp.clip(row - start, 0, 30)) & 1

    for at in range(0, keys_ref.shape[1], 2 * TILE):
        n = 2 * TILE
        seg, var, time, gone = (keys_ref[i : i + 1, at : at + n] for i in range(4))
        row = lax.broadcasted_iota(I32, (128, n), 0)
        late = jnp.where(time > row, 1, 0)
        outside = jnp.where(row == last, gone, 0)
        off = jnp.where(row < bit0, late, jnp.where(row < bit1, bit(seg, row, bit0), 0))
        off = jnp.where((row >= bit1) & (row < last), 1 - bit(seg, row, bit1), off) + outside
        fk_ref[at : at + n, :] = (off.astype(F32) * -BIG).T.astype(BF16)
        vk_ref[at : at + n, :] = jnp.broadcast_to(var, (128, n)).T
    for at in range(0, asks_ref.shape[1], 2 * TILE):
        n = 2 * TILE
        seg, time = asks_ref[0:1, at : at + n], asks_ref[1:2, at : at + n]
        row = lax.broadcasted_iota(I32, (128, n), 0)
        on = jnp.where(row < bit0, jnp.where(time == row, 1, 0), jnp.where(row < bit1, 1 - bit(seg, row, bit0), 0))
        on = jnp.where((row >= bit1) & (row < last), bit(seg, row, bit1), on) + jnp.where(row == last, 1, 0)
        fqt_ref[:, at : at + n] = on.astype(F32).astype(BF16)


def attend_kernel(
    hsize, q0, nq, tab_ref, delta_ref, k_ref, vt_ref, qt_ref, fk_ref, fqt_ref, vk_ref, vq_ref, o_ref, qa0, qa1, sc0, sc1, m0, m1
):
    qi = pl.program_id(0)
    qas, scs, ms = (qa0, qa1), (sc0, sc1), (m0, m1)
    nt = sc0.shape[0]
    wide = nt + 1
    two = 2 * hsize

    def place(q, kk):
        return pl.multiple_of(tab_ref[(q0 + q) * wide + kk], TILE)

    def lanes(q):
        return pl.ds(pl.multiple_of((q0 + q) * TILE, TILE), TILE)

    def prep():
        zero = jnp.zeros((hsize, TILE), BF16)
        for j, qa in enumerate(qas):
            qa[0:hsize, 0:TILE] = qt_ref[two * j : two * j + hsize, lanes(qi)]
            qa[0:hsize, TILE:] = zero
            qa[hsize:two, 0:TILE] = zero
            qa[hsize:two, TILE:] = qt_ref[two * j + hsize : two * (j + 1), lanes(qi)]
            f = fqt_ref[:, lanes(qi)]
            qa[two:, 0:TILE] = f
            qa[two:, TILE:] = f

    def scores(j, kk, share, m):
        at = place(qi, kk)
        lhs = jnp.concatenate([k_ref[pl.ds(at, TILE), two * j : two * (j + 1)], fk_ref[pl.ds(at, TILE), :]], axis=1)
        s = jnp.dot(lhs, qas[j][...], preferred_element_type=F32)
        if kk in (0, nt - 1):
            r = lax.broadcasted_iota(I32, (TILE, TILE), 0)
            p = lax.broadcasted_iota(I32, (TILE, TILE), 1)
            ok = (r > p) if kk == 0 else (r < p)
            s = jnp.where(jnp.concatenate([ok, ok], axis=1), s, -BIG)
        if share:
            vk = vk_ref[pl.ds(at, TILE), :]
            same = jnp.concatenate([vk, vk], axis=1) == vq_ref[:, lanes(qi)]
            s = s + jnp.concatenate(
                [jnp.where(same, delta_ref[2 * j], 0.0), jnp.where(same, delta_ref[2 * j + 1], 0.0)], axis=1
            )
        scs[j][kk] = s
        return jnp.maximum(m, jnp.max(s.reshape(TILE // 8, 8, 2 * TILE), axis=0))

    def mix(j, q, kk, top, state):
        tot, oa, ob = state
        vt = vt_ref[two * j : two * (j + 1), pl.ds(place(q, kk), TILE)]
        w = jnp.exp2((scs[j][kk] - top) * LOG2E)
        tot = tot + jnp.sum(w.reshape(TILE // 8, 8, 2 * TILE), axis=0)
        wb = w.astype(BF16)
        oa = oa + jnp.dot(vt[:hsize], wb[:, :TILE], preferred_element_type=F32)
        ob = ob + jnp.dot(vt[hsize:], wb[:, TILE:], preferred_element_type=F32)
        return tot, oa, ob

    def phase(j, old, q, share):
        m = jnp.full((8, 2 * TILE), -BIG, F32)
        z = jnp.zeros((hsize, TILE), F32)
        state = (jnp.zeros((8, 2 * TILE), F32), z, z)
        if old is not None:
            top = jnp.max(ms[old][...], axis=0, keepdims=True)
        for kk in range(nt):
            if j is not None:
                m = scores(j, kk, share or abs(kk - nt // 2) <= 1, m)
            if old is not None:
                state = mix(old, q, kk, top, state)
        if j is not None:
            ms[j][...] = m
        if old is not None:
            tot, oa, ob = state
            tot = jnp.sum(tot, axis=0, keepdims=True)
            o = jnp.concatenate([oa / tot[:, :TILE], ob / tot[:, TILE:]], axis=0)
            o_ref[pl.ds(pl.multiple_of(q * TILE, TILE), TILE), two * old : two * (old + 1)] = o.T.astype(BF16)

    prep()
    far = tab_ref[(q0 + qi) * wide + nt]
    for share in (False, True):

        @pl.when((far != 0) == share)
        def _(share=share):
            @pl.when(qi == 0)
            def _():
                phase(0, None, 0, share)

            @pl.when(qi > 0)
            def _():
                phase(0, 1, qi - 1, share)

            phase(1, 0, qi, share)

    @pl.when(qi == nq - 1)
    def _():
        phase(None, 1, qi, False)


def out_kernel(planes, who_ref, a0, a1, a2, a3, w0, w1, w2, o_ref, w):
    me, plane = who_ref[0], who_ref[1]
    for part, place in ((w0, me), (w1.at[0], me ^ 1), (w2, me ^ 2), (w1.at[1], me ^ 3)):
        rows = part.shape[0] // planes
        for i in range(planes):
            source = lax.rem(plane + planes - i, planes)
            at = pl.multiple_of((4 * source + place) * rows, rows)
            w[pl.ds(at, rows), :] = part[i * rows : (i + 1) * rows, :]
    total = None
    for a, place in ((a0, me), (a1, me ^ 1), (a2, me ^ 2), (a3, me ^ 3)):
        cols = a.shape[1]
        part = jnp.dot(a[...], w[pl.ds(pl.multiple_of(place * cols, cols), cols), :], preferred_element_type=F32)
        total = part if total is None else total + part
    o_ref[...] = total.astype(BF16)


def in_plane(blocks):
    swap = [(0, 1), (1, 0)]
    cross = [(0, 3), (1, 2), (2, 1), (3, 0)]
    return [
        lax.ppermute(blocks[0], "core", swap),
        lax.ppermute(blocks[1], "side", swap),
        lax.ppermute(blocks[2], ("side", "core"), cross),
    ]


def work(micros):
    return pl.CostEstimate(flops=int(micros * 1.1e9), transcendentals=0, bytes_accessed=1 << 20)


def turns(block, planes):
    return [block] + [
        lax.ppermute(block, "plane", [(i, (i + s) % planes) for i in range(planes)]) for s in range(1, planes)
    ]


def local(groups, planes, tokens, w_qkv, w_out, var_bias, seg_id, var_id, time_id):
    rows, width = tokens.shape
    heads = var_bias.shape[1]
    hsize = width // heads
    cols = width // 4
    core = lax.axis_index("core")
    side = lax.axis_index("side")
    plane = lax.axis_index("plane")
    swap = [(0, 1), (1, 0)]
    cross = [(0, 3), (1, 2), (2, 1), (3, 0)]
    pair = ("plane", "side")
    native, passed, direct = [], [], []
    for p in range(planes - 1):
        native += [(2 * (p + 1), 2 * p), (2 * p + 1, 2 * (p + 1) + 1)]
        passed += [(2 * p, 2 * (p + 1)), (2 * (p + 1) + 1, 2 * p + 1)]
        direct += [(2 * p + 1, 2 * (p + 1)), (2 * (p + 1), 2 * p + 1)]

    group = lax.axis_index("groups")
    me = 2 * side + core
    wide = cols // 2
    mate = [(g, g ^ 1) for g in range(groups)]
    couple = groups % 2 == 0
    picked = pl.pallas_call(
        functools.partial(pick_kernel, width, cols, wide, 1 if couple else 2),
        out_shape=[jax.ShapeDtypeStruct((w_qkv.shape[0], (3 if couple else 6) * wide), BF16)] * 4,
        in_specs=[pl.BlockSpec(memory_space=pltpu.SMEM), pl.BlockSpec(memory_space=pltpu.VMEM)],
        out_specs=[pl.BlockSpec(memory_space=pltpu.VMEM)] * 4,
        cost_estimate=work(1),
        name="pick",
    )(jnp.stack([me, group % 2]).astype(I32), w_qkv)
    came = in_plane(picked[1:])
    plane_w = jnp.concatenate([picked[0]] + came, 0)
    w_parts = turns(plane_w, planes)
    turned = w_parts[1:]
    half_w = jnp.concatenate(w_parts, 0)
    if couple:
        w_parts = [half_w, lax.ppermute(half_w, "groups", mate)]
    else:
        w_parts = [half_w]

    cut = rows // 2
    tokens = lax.optimization_barrier((tokens, picked))[0]
    digits = jnp.stack([seg_id, var_id >> 4, var_id & 15, time_id], 0).astype(BF16).reshape(4 * rows // width, width)
    digits = jnp.pad(digits, ((0, ID_ROWS - digits.shape[0]), (0, 0)))
    first = jnp.concatenate([tokens[:cut], digits], 0)
    whole = jnp.concatenate([tokens, digits], 0)
    first, second, _ = lax.optimization_barrier((first, tokens[cut:], came))
    other = [lax.ppermute(x, "side", swap) for x in (first, second)]
    first_z = lax.optimization_barrier((first, turned))[0]
    mine = [lax.ppermute(first_z, pair, native)]
    theirs = [lax.ppermute(other[0], pair, passed)]
    whole, second, passing, _, _ = lax.optimization_barrier(
        (whole, second, other[1], (mine[0], theirs[0]), w_parts)
    )
    mine.append(lax.ppermute(second, pair, native))
    theirs.append(lax.ppermute(passing, pair, passed))
    other[1] = passing
    peers = [lax.ppermute(x, "core", swap) for x in (whole, other[0], mine[0], theirs[0])]

    def ids_of(x, n):
        return x[n : n + 4 * rows // width].reshape(4, rows).astype(I32)

    ids = [ids_of(x, cut) for x in (other[0], mine[0], theirs[0])]
    ids += [ids_of(peers[0], rows)] + [ids_of(x, cut) for x in peers[1:]]
    seg, hi, lo, time = jnp.concatenate([ids_of(digits, 0)] + ids, 1)
    var = hi * 16 + lo

    nk = 8 * rows
    per = rows // TILE
    nt = 4 * per + 1
    nq = 2 * per
    below = jnp.where(side == 0, 3, 2)
    stream = jnp.arange(4, dtype=I32)
    there = jnp.where(stream == below, plane > 0, jnp.where(stream == 5 - below, plane < planes - 1, True))
    there = jnp.tile(there, 2)
    gone = jnp.repeat(~there, rows).astype(I32)

    def asked(a):
        return jnp.concatenate([a[0:rows], a[4 * rows : 5 * rows], a[rows : 2 * rows], a[5 * rows : 6 * rows]], 0)

    var_q = asked(var)
    keys_ids = jnp.stack([seg, var, time, gone], 0)
    vm = pl.BlockSpec(memory_space=pltpu.VMEM)
    fk, vk, fqt = pl.pallas_call(
        mask_kernel,
        out_shape=[
            jax.ShapeDtypeStruct((nk, 128), BF16),
            jax.ShapeDtypeStruct((nk, 128), I32),
            jax.ShapeDtypeStruct((128, 4 * rows), BF16),
        ],
        in_specs=[vm] * 2,
        out_specs=[vm] * 3,
        cost_estimate=work(2),
        name="masks",
    )(keys_ids, jnp.stack([asked(seg), asked(time)], 0))

    qtile = jnp.arange(4 * per, dtype=I32)
    qblock = qtile // per
    q_side = jnp.where(qblock // 2 == 0, side, 1 - side)
    q_core = jnp.where(qblock % 2 == 0, core, 1 - core)
    q_win = (2 + 2 * q_side + q_core) * per + qtile % per
    k_win = q_win[:, None] - 2 * per + jnp.arange(nt, dtype=I32)[None, :]
    k_block = k_win // per
    k_token = k_block // 2
    k_stream = jnp.where(
        side == 0,
        jnp.where(k_token == 0, 3, k_token - 1),
        jnp.where(k_token == 3, 3, 2 - k_token),
    )
    k_place = (jnp.where(k_block % 2 == core, 0, 4) + k_stream) * per + k_win % per
    code = (seg * 1024 + var).reshape(nk // TILE, TILE)
    lo, hi = code.min(1), code.max(1)
    tile = jnp.arange(8 * per, dtype=I32)
    t_block = tile // per
    t_core = jnp.where(t_block // 4 == 0, core, 1 - core)
    t_stream = t_block % 4
    t_token = jnp.where(side == 0, (t_stream + 1) % 4, jnp.where(t_stream == 3, 3, 2 - t_stream))
    apart = ((2 * t_token + t_core) * per + tile % per)[None, :] - q_win[:, None]
    apart = jnp.abs(apart)
    hi_q = jnp.concatenate([hi[b * per : (b + 1) * per] for b in (0, 4, 1, 5)])
    lo_q = jnp.concatenate([lo[b * per : (b + 1) * per] for b in (0, 4, 1, 5)])
    share = (lo[None, :] <= hi_q[:, None]) & (hi[None, :] >= lo_q[:, None])
    share = share & jnp.repeat(there, per)[None, :] & (apart > 1) & (apart <= nt // 2)
    table = jnp.concatenate([k_place * TILE, share.any(1, keepdims=True).astype(I32)], 1).reshape(-1)
    delta = lax.dynamic_slice_in_dim(var_bias[0] - var_bias[1], (2 * side + core) * (heads // 4), heads // 4, 0)

    who = jnp.stack([me, plane, group % 2]).astype(I32)
    masks = (fk, fqt, vk, table)
    rest = [lax.ppermute(passing, "core", swap)]
    lasts, masks = lax.optimization_barrier(((mine[1], theirs[1]), masks))
    fk, fqt, vk, table = masks
    rest += [lax.ppermute(x, "core", swap) for x in lasts]
    held = [(0, rows, tokens), (4 * rows, rows, peers[0])]
    for i, (one, two) in enumerate((other, (mine[0], lasts[0]), (theirs[0], lasts[1]))):
        held += [((i + 1) * rows, cut, one), ((i + 1) * rows + cut, cut, two)]
        held += [((i + 5) * rows, cut, peers[i + 1]), ((i + 5) * rows + cut, cut, rest[i])]
    plan = tuple((at, n) for at, n, _ in held)
    xs = [x for _, _, x in held]
    limit = pltpu.CompilerParams(vmem_limit_bytes=48 << 20)
    queries = {}
    for at, _ in plan:
        block = at // rows
        if block in (0, 1, 4, 5):
            queries[at] = {0: 0, 4: rows, 1: 2 * rows, 5: 3 * rows}[block] + at % rows
    k, vt, qt = pl.pallas_call(
        functools.partial(project_kernel, cols, plan, queries, planes, couple),
        out_shape=[
            jax.ShapeDtypeStruct((nk, cols), BF16),
            jax.ShapeDtypeStruct((cols, nk), BF16),
            jax.ShapeDtypeStruct((cols, 4 * rows), BF16),
        ],
        in_specs=[pl.BlockSpec(memory_space=pltpu.SMEM)] + [vm] * (len(xs) + len(w_parts)),
        out_specs=[vm] * 3,
        scratch_shapes=[pltpu.VMEM((width, 3 * cols), BF16)],
        compiler_params=limit,
        cost_estimate=work(12),
        name="project",
    )(who, *xs, *w_parts)

    late_w = lax.optimization_barrier((w_out, lasts))[0]
    wo = turns(late_w, planes)

    def attend(q0):
        return pl.pallas_call(
            functools.partial(attend_kernel, hsize, q0, nq),
            out_shape=jax.ShapeDtypeStruct((2 * rows, cols), BF16),
            grid_spec=pltpu.PrefetchScalarGridSpec(
                num_scalar_prefetch=2,
                grid=(nq,),
                in_specs=[vm] * 7,
                out_specs=vm,
                scratch_shapes=[pltpu.VMEM((2 * hsize + 128, 2 * TILE), BF16)] * 2
                + [pltpu.VMEM((nt, TILE, 2 * TILE), F32)] * 2
                + [pltpu.VMEM((8, 2 * TILE), F32)] * 2,
            ),
            compiler_params=limit,
            cost_estimate=work(16),
            name="attend",
        )(table, delta, k, vt, qt, fk, fqt, vk, var_q[None, :])

    far = attend(nq)
    far_side, far_cross = far[:rows], far[rows:]
    wo, far_side, far_cross = lax.optimization_barrier((wo, far_side, far_cross))
    wo = jnp.concatenate(wo, 0)
    far_side = lax.ppermute(far_side, "side", swap)
    far_cross = lax.ppermute(far_cross, ("side", "core"), cross)
    wo_side = lax.ppermute(wo, "side", swap)
    near = attend(0)
    near_core, near = near[rows:], near[:rows]
    near_core, far_side, far_cross, wo_side = lax.optimization_barrier((near_core, far_side, far_cross, wo_side))
    near_core = lax.ppermute(near_core, "core", swap)
    wo_core = lax.ppermute(jnp.stack([wo, wo_side]), "core", swap)
    wo_parts = [wo, wo_core, wo_side]
    return pl.pallas_call(
        functools.partial(out_kernel, planes),
        out_shape=jax.ShapeDtypeStruct((rows, width), BF16),
        in_specs=[pl.BlockSpec(memory_space=pltpu.SMEM)] + [vm] * 7,
        out_specs=vm,
        scratch_shapes=[pltpu.VMEM((width, width), BF16)],
        compiler_params=limit,
        cost_estimate=work(3),
        name="mixed",
    )(jnp.stack([me, plane]).astype(I32), near, near_core, far_side, far_cross, *wo_parts)


def solution(mesh):
    groups, ctx = mesh.shape["groups"], mesh.shape["ctx"]
    planes = ctx // 4
    mesh4 = Mesh(mesh.devices.reshape(groups, planes, 2, 2), ("groups", "plane", "side", "core"))
    toks = ("groups", "plane", "side", "core")
    par = ("plane", "side", "core")
    in_specs = (P(toks, None), P(par, None), P(par, None), P(), P(toks), P(toks), P(toks))
    return jax.shard_map(
        functools.partial(local, groups, planes), mesh=mesh4, in_specs=in_specs, out_specs=P(toks, None), check_vma=False
    )
```

```python
import functools
import math

import jax
import jax.numpy as jnp
from jax import lax
from jax.experimental import pallas as pl
from jax.experimental.pallas import tpu as pltpu
from jax.sharding import Mesh, PartitionSpec as P

BIG = 2.0**100
TIMES = 104
SEG_BITS = 8
TILE = 256
ID_ROWS = 16
LOG2E = math.log2(math.e)
F32 = jnp.float32
BF16 = jnp.bfloat16
I32 = jnp.int32


def pick_kernel(width, cols, wide, pairs, who_ref, w_ref, *outs):
    me, half = who_ref[0], who_ref[1]
    for step, out in enumerate(outs):
        to = me ^ step
        for a in range(3):
            for b in range(pairs):
                at = pl.multiple_of(a * width + to * cols + (half ^ b if pairs == 1 else b) * wide, wide)
                out[:, (a * pairs + b) * wide : (a * pairs + b + 1) * wide] = w_ref[:, pl.ds(at, wide)]


def project_kernel(cols, plan, queries, planes, couple, who_ref, *refs):
    n = len(plan)
    k_ref, vt_ref, qt_ref, w = refs[-4:]
    xs, parts = refs[:n], refs[n:-4]
    me, plane, half = who_ref[0], who_ref[1], who_ref[2]
    wide = cols // 2
    rows = w.shape[0] // (4 * planes)
    for i, part in enumerate(parts):
        pair = half if i == 0 else 1 - half
        for p in range(planes):
            source = lax.rem(plane + planes - p, planes)
            for step in range(4):
                to = pl.multiple_of((4 * source + (me ^ step)) * rows, rows)
                block = part[(4 * p + step) * rows : (4 * p + step + 1) * rows, :]
                if couple:
                    for a in range(3):
                        at = pl.multiple_of(a * cols + pair * wide, wide)
                        w[pl.ds(to, rows), pl.ds(at, wide)] = block[:, a * wide : (a + 1) * wide]
                else:
                    w[pl.ds(to, rows), :] = block
    for x, (at, rows) in zip(xs, plan):
        out = jnp.dot(x[0:rows, :], w[:, cols:], preferred_element_type=F32)
        k_ref[at : at + rows, :] = out[:, :cols].astype(BF16)
        vt_ref[:, at : at + rows] = out[:, cols:].astype(BF16).T
        if at in queries:
            out = jnp.dot(x[0:rows, :], w[:, :cols], preferred_element_type=F32)
            q = (out.astype(BF16) * 0.125).astype(BF16)
            qt_ref[:, queries[at] : queries[at] + rows] = q.T


def mask_kernel(keys_ref, asks_ref, fk_ref, vk_ref, fqt_ref):
    bit0, bit1, last = TIMES, TIMES + SEG_BITS, TIMES + 2 * SEG_BITS

    def bit(seg, row, start):
        return (seg >> jnp.clip(row - start, 0, 30)) & 1

    for at in range(0, keys_ref.shape[1], 2 * TILE):
        n = 2 * TILE
        seg, var, time, gone = (keys_ref[i : i + 1, at : at + n] for i in range(4))
        row = lax.broadcasted_iota(I32, (128, n), 0)
        late = jnp.where(time > row, 1, 0)
        outside = jnp.where(row == last, gone, 0)
        off = jnp.where(row < bit0, late, jnp.where(row < bit1, bit(seg, row, bit0), 0))
        off = jnp.where((row >= bit1) & (row < last), 1 - bit(seg, row, bit1), off) + outside
        fk_ref[at : at + n, :] = (off.astype(F32) * -BIG).T.astype(BF16)
        vk_ref[at : at + n, :] = jnp.broadcast_to(var, (128, n)).T
    for at in range(0, asks_ref.shape[1], 2 * TILE):
        n = 2 * TILE
        seg, time = asks_ref[0:1, at : at + n], asks_ref[1:2, at : at + n]
        row = lax.broadcasted_iota(I32, (128, n), 0)
        on = jnp.where(row < bit0, jnp.where(time == row, 1, 0), jnp.where(row < bit1, 1 - bit(seg, row, bit0), 0))
        on = jnp.where((row >= bit1) & (row < last), bit(seg, row, bit1), on) + jnp.where(row == last, 1, 0)
        fqt_ref[:, at : at + n] = on.astype(F32).astype(BF16)


def attend_kernel(
    hsize, q0, nq, tab_ref, delta_ref, k_ref, vt_ref, qt_ref, fk_ref, fqt_ref, vk_ref, vq_ref, o_ref, qa0, qa1, sc0, sc1, m0, m1
):
    qi = pl.program_id(0)
    qas, scs, ms = (qa0, qa1), (sc0, sc1), (m0, m1)
    nt = sc0.shape[0]
    wide = nt + 1
    two = 2 * hsize

    def place(q, kk):
        return pl.multiple_of(tab_ref[(q0 + q) * wide + kk], TILE)

    def lanes(q):
        return pl.ds(pl.multiple_of((q0 + q) * TILE, TILE), TILE)

    def prep():
        zero = jnp.zeros((hsize, TILE), BF16)
        for j, qa in enumerate(qas):
            qa[0:hsize, 0:TILE] = qt_ref[two * j : two * j + hsize, lanes(qi)]
            qa[0:hsize, TILE:] = zero
            qa[hsize:two, 0:TILE] = zero
            qa[hsize:two, TILE:] = qt_ref[two * j + hsize : two * (j + 1), lanes(qi)]
            f = fqt_ref[:, lanes(qi)]
            qa[two:, 0:TILE] = f
            qa[two:, TILE:] = f

    def scores(j, kk, share, m):
        at = place(qi, kk)
        lhs = jnp.concatenate([k_ref[pl.ds(at, TILE), two * j : two * (j + 1)], fk_ref[pl.ds(at, TILE), :]], axis=1)
        s = jnp.dot(lhs, qas[j][...], preferred_element_type=F32)
        if kk in (0, nt - 1):
            r = lax.broadcasted_iota(I32, (TILE, TILE), 0)
            p = lax.broadcasted_iota(I32, (TILE, TILE), 1)
            ok = (r > p) if kk == 0 else (r < p)
            s = jnp.where(jnp.concatenate([ok, ok], axis=1), s, -BIG)
        if share:
            vk = vk_ref[pl.ds(at, TILE), :]
            same = jnp.concatenate([vk, vk], axis=1) == vq_ref[:, lanes(qi)]
            s = s + jnp.concatenate(
                [jnp.where(same, delta_ref[2 * j], 0.0), jnp.where(same, delta_ref[2 * j + 1], 0.0)], axis=1
            )
        scs[j][kk] = s
        return jnp.maximum(m, jnp.max(s.reshape(TILE // 8, 8, 2 * TILE), axis=0))

    def mix(j, q, kk, top, state):
        tot, oa, ob = state
        vt = vt_ref[two * j : two * (j + 1), pl.ds(place(q, kk), TILE)]
        w = jnp.exp2((scs[j][kk] - top) * LOG2E)
        tot = tot + jnp.sum(w.reshape(TILE // 8, 8, 2 * TILE), axis=0)
        wb = w.astype(BF16)
        oa = oa + jnp.dot(vt[:hsize], wb[:, :TILE], preferred_element_type=F32)
        ob = ob + jnp.dot(vt[hsize:], wb[:, TILE:], preferred_element_type=F32)
        return tot, oa, ob

    def phase(j, old, q, share):
        m = jnp.full((8, 2 * TILE), -BIG, F32)
        z = jnp.zeros((hsize, TILE), F32)
        state = (jnp.zeros((8, 2 * TILE), F32), z, z)
        if old is not None:
            top = jnp.max(ms[old][...], axis=0, keepdims=True)
        for kk in range(nt):
            if j is not None:
                m = scores(j, kk, share or abs(kk - nt // 2) <= 1, m)
            if old is not None:
                state = mix(old, q, kk, top, state)
        if j is not None:
            ms[j][...] = m
        if old is not None:
            tot, oa, ob = state
            tot = jnp.sum(tot, axis=0, keepdims=True)
            o = jnp.concatenate([oa / tot[:, :TILE], ob / tot[:, TILE:]], axis=0)
            o_ref[pl.ds(pl.multiple_of(q * TILE, TILE), TILE), two * old : two * (old + 1)] = o.T.astype(BF16)

    prep()
    far = tab_ref[(q0 + qi) * wide + nt]
    for share in (False, True):

        @pl.when((far != 0) == share)
        def _(share=share):
            @pl.when(qi == 0)
            def _():
                phase(0, None, 0, share)

            @pl.when(qi > 0)
            def _():
                phase(0, 1, qi - 1, share)

            phase(1, 0, qi, share)

    @pl.when(qi == nq - 1)
    def _():
        phase(None, 1, qi, False)


def out_kernel(planes, who_ref, a0, a1, a2, a3, w0, w1, w2, o_ref, w):
    me, plane = who_ref[0], who_ref[1]
    for part, place in ((w0, me), (w1.at[0], me ^ 1), (w2, me ^ 2), (w1.at[1], me ^ 3)):
        rows = part.shape[0] // planes
        for i in range(planes):
            source = lax.rem(plane + planes - i, planes)
            at = pl.multiple_of((4 * source + place) * rows, rows)
            w[pl.ds(at, rows), :] = part[i * rows : (i + 1) * rows, :]
    total = None
    for a, place in ((a0, me), (a1, me ^ 1), (a2, me ^ 2), (a3, me ^ 3)):
        cols = a.shape[1]
        part = jnp.dot(a[...], w[pl.ds(pl.multiple_of(place * cols, cols), cols), :], preferred_element_type=F32)
        total = part if total is None else total + part
    o_ref[...] = total.astype(BF16)


def in_plane(blocks):
    swap = [(0, 1), (1, 0)]
    cross = [(0, 3), (1, 2), (2, 1), (3, 0)]
    return [
        lax.ppermute(blocks[0], "core", swap),
        lax.ppermute(blocks[1], "side", swap),
        lax.ppermute(blocks[2], ("side", "core"), cross),
    ]


def work(micros):
    return pl.CostEstimate(flops=int(micros * 1.1e9), transcendentals=0, bytes_accessed=1 << 20)


def turns(block, planes):
    return [block] + [
        lax.ppermute(block, "plane", [(i, (i + s) % planes) for i in range(planes)]) for s in range(1, planes)
    ]


def local(groups, planes, tokens, w_qkv, w_out, var_bias, seg_id, var_id, time_id):
    rows, width = tokens.shape
    heads = var_bias.shape[1]
    hsize = width // heads
    cols = width // 4
    core = lax.axis_index("core")
    side = lax.axis_index("side")
    plane = lax.axis_index("plane")
    swap = [(0, 1), (1, 0)]
    cross = [(0, 3), (1, 2), (2, 1), (3, 0)]
    pair = ("plane", "side")
    native, passed, direct = [], [], []
    for p in range(planes - 1):
        native += [(2 * (p + 1), 2 * p), (2 * p + 1, 2 * (p + 1) + 1)]
        passed += [(2 * p, 2 * (p + 1)), (2 * (p + 1) + 1, 2 * p + 1)]
        direct += [(2 * p + 1, 2 * (p + 1)), (2 * (p + 1), 2 * p + 1)]

    group = lax.axis_index("groups")
    me = 2 * side + core
    wide = cols // 2
    mate = [(g, g ^ 1) for g in range(groups)]
    couple = groups % 2 == 0
    picked = pl.pallas_call(
        functools.partial(pick_kernel, width, cols, wide, 1 if couple else 2),
        out_shape=[jax.ShapeDtypeStruct((w_qkv.shape[0], (3 if couple else 6) * wide), BF16)] * 4,
        in_specs=[pl.BlockSpec(memory_space=pltpu.SMEM), pl.BlockSpec(memory_space=pltpu.VMEM)],
        out_specs=[pl.BlockSpec(memory_space=pltpu.VMEM)] * 4,
        cost_estimate=work(1),
        name="pick",
    )(jnp.stack([me, group % 2]).astype(I32), w_qkv)
    came = in_plane(picked[1:])
    plane_w = jnp.concatenate([picked[0]] + came, 0)
    w_parts = turns(plane_w, planes)
    turned = w_parts[1:]
    half_w = jnp.concatenate(w_parts, 0)
    if couple:
        w_parts = [half_w, lax.ppermute(half_w, "groups", mate)]
    else:
        w_parts = [half_w]

    cut = rows // 2
    tokens = lax.optimization_barrier((tokens, picked))[0]
    digits = jnp.stack([seg_id, var_id >> 4, var_id & 15, time_id], 0).astype(BF16).reshape(4 * rows // width, width)
    digits = jnp.pad(digits, ((0, ID_ROWS - digits.shape[0]), (0, 0)))
    first = jnp.concatenate([tokens[:cut], digits], 0)
    whole = jnp.concatenate([tokens, digits], 0)
    wo = turns(lax.optimization_barrier((w_out, picked))[0], planes)
    first, second, _, wo = lax.optimization_barrier((first, tokens[cut:], came, wo))
    other = [lax.ppermute(x, "side", swap) for x in (first, second)]
    first_z = lax.optimization_barrier((first, turned))[0]
    mine = [lax.ppermute(first_z, pair, native)]
    theirs = [lax.ppermute(other[0], pair, passed)]
    whole, second, passing, _, _ = lax.optimization_barrier(
        (whole, second, other[1], (mine[0], theirs[0]), w_parts)
    )
    mine.append(lax.ppermute(second, pair, native))
    theirs.append(lax.ppermute(passing, pair, passed))
    other[1] = passing
    peers = [lax.ppermute(x, "core", swap) for x in (whole, other[0], mine[0], theirs[0])]

    def ids_of(x, n):
        return x[n : n + 4 * rows // width].reshape(4, rows).astype(I32)

    ids = [ids_of(x, cut) for x in (other[0], mine[0], theirs[0])]
    ids += [ids_of(peers[0], rows)] + [ids_of(x, cut) for x in peers[1:]]
    seg, hi, lo, time = jnp.concatenate([ids_of(digits, 0)] + ids, 1)
    var = hi * 16 + lo

    nk = 8 * rows
    per = rows // TILE
    nt = 4 * per + 1
    nq = 2 * per
    below = jnp.where(side == 0, 3, 2)
    stream = jnp.arange(4, dtype=I32)
    there = jnp.where(stream == below, plane > 0, jnp.where(stream == 5 - below, plane < planes - 1, True))
    there = jnp.tile(there, 2)
    gone = jnp.repeat(~there, rows).astype(I32)

    def asked(a):
        return jnp.concatenate([a[0:rows], a[4 * rows : 5 * rows], a[rows : 2 * rows], a[5 * rows : 6 * rows]], 0)

    var_q = asked(var)
    keys_ids = jnp.stack([seg, var, time, gone], 0)
    vm = pl.BlockSpec(memory_space=pltpu.VMEM)
    fk, vk, fqt = pl.pallas_call(
        mask_kernel,
        out_shape=[
            jax.ShapeDtypeStruct((nk, 128), BF16),
            jax.ShapeDtypeStruct((nk, 128), I32),
            jax.ShapeDtypeStruct((128, 4 * rows), BF16),
        ],
        in_specs=[vm] * 2,
        out_specs=[vm] * 3,
        cost_estimate=work(2),
        name="masks",
    )(keys_ids, jnp.stack([asked(seg), asked(time)], 0))

    qtile = jnp.arange(4 * per, dtype=I32)
    qblock = qtile // per
    q_side = jnp.where(qblock // 2 == 0, side, 1 - side)
    q_core = jnp.where(qblock % 2 == 0, core, 1 - core)
    q_win = (2 + 2 * q_side + q_core) * per + qtile % per
    k_win = q_win[:, None] - 2 * per + jnp.arange(nt, dtype=I32)[None, :]
    k_block = k_win // per
    k_token = k_block // 2
    k_stream = jnp.where(
        side == 0,
        jnp.where(k_token == 0, 3, k_token - 1),
        jnp.where(k_token == 3, 3, 2 - k_token),
    )
    k_place = (jnp.where(k_block % 2 == core, 0, 4) + k_stream) * per + k_win % per
    code = (seg * 1024 + var).reshape(nk // TILE, TILE)
    lo, hi = code.min(1), code.max(1)
    tile = jnp.arange(8 * per, dtype=I32)
    t_block = tile // per
    t_core = jnp.where(t_block // 4 == 0, core, 1 - core)
    t_stream = t_block % 4
    t_token = jnp.where(side == 0, (t_stream + 1) % 4, jnp.where(t_stream == 3, 3, 2 - t_stream))
    apart = ((2 * t_token + t_core) * per + tile % per)[None, :] - q_win[:, None]
    apart = jnp.abs(apart)
    hi_q = jnp.concatenate([hi[b * per : (b + 1) * per] for b in (0, 4, 1, 5)])
    lo_q = jnp.concatenate([lo[b * per : (b + 1) * per] for b in (0, 4, 1, 5)])
    share = (lo[None, :] <= hi_q[:, None]) & (hi[None, :] >= lo_q[:, None])
    share = share & jnp.repeat(there, per)[None, :] & (apart > 1) & (apart <= nt // 2)
    table = jnp.concatenate([k_place * TILE, share.any(1, keepdims=True).astype(I32)], 1).reshape(-1)
    delta = lax.dynamic_slice_in_dim(var_bias[0] - var_bias[1], (2 * side + core) * (heads // 4), heads // 4, 0)

    who = jnp.stack([me, plane, group % 2]).astype(I32)
    masks = (fk, fqt, vk, table)
    rest = [lax.ppermute(passing, "core", swap)]
    lasts, masks = lax.optimization_barrier(((mine[1], theirs[1]), masks))
    fk, fqt, vk, table = masks
    rest += [lax.ppermute(x, "core", swap) for x in lasts]
    held = [(0, rows, tokens), (4 * rows, rows, peers[0])]
    for i, (one, two) in enumerate((other, (mine[0], lasts[0]), (theirs[0], lasts[1]))):
        held += [((i + 1) * rows, cut, one), ((i + 1) * rows + cut, cut, two)]
        held += [((i + 5) * rows, cut, peers[i + 1]), ((i + 5) * rows + cut, cut, rest[i])]
    plan = tuple((at, n) for at, n, _ in held)
    xs = [x for _, _, x in held]
    limit = pltpu.CompilerParams(vmem_limit_bytes=28 << 20)
    queries = {}
    for at, _ in plan:
        block = at // rows
        if block in (0, 1, 4, 5):
            queries[at] = {0: 0, 4: rows, 1: 2 * rows, 5: 3 * rows}[block] + at % rows
    k, vt, qt = pl.pallas_call(
        functools.partial(project_kernel, cols, plan, queries, planes, couple),
        out_shape=[
            jax.ShapeDtypeStruct((nk, cols), BF16),
            jax.ShapeDtypeStruct((cols, nk), BF16),
            jax.ShapeDtypeStruct((cols, 4 * rows), BF16),
        ],
        in_specs=[pl.BlockSpec(memory_space=pltpu.SMEM)] + [vm] * (len(xs) + len(w_parts)),
        out_specs=[vm] * 3,
        scratch_shapes=[pltpu.VMEM((width, 3 * cols), BF16)],
        compiler_params=limit,
        cost_estimate=work(12),
        name="project",
    )(who, *xs, *w_parts)

    wo, k, vt, qt = lax.optimization_barrier((jnp.concatenate(wo, 0), k, vt, qt))
    wo_side = lax.ppermute(wo, "side", swap)

    def attend(q0):
        return pl.pallas_call(
            functools.partial(attend_kernel, hsize, q0, nq),
            out_shape=jax.ShapeDtypeStruct((2 * rows, cols), BF16),
            grid_spec=pltpu.PrefetchScalarGridSpec(
                num_scalar_prefetch=2,
                grid=(nq,),
                in_specs=[vm] * 7,
                out_specs=vm,
                scratch_shapes=[pltpu.VMEM((2 * hsize + 128, 2 * TILE), BF16)] * 2
                + [pltpu.VMEM((nt, TILE, 2 * TILE), F32)] * 2
                + [pltpu.VMEM((8, 2 * TILE), F32)] * 2,
            ),
            compiler_params=limit,
            cost_estimate=work(16),
            name="attend",
        )(table, delta, k, vt, qt, fk, fqt, vk, var_q[None, :])

    far = attend(nq)
    far_side, far_cross, wo_side = lax.optimization_barrier((far[:rows], far[rows:], wo_side))
    far_side = lax.ppermute(far_side, "side", swap)
    far_cross = lax.ppermute(far_cross, ("side", "core"), cross)
    wo_core = lax.ppermute(jnp.stack([wo, wo_side]), "core", swap)
    near = attend(0)
    near_core, near = near[rows:], near[:rows]
    near_core, far_side, far_cross, wo_core = lax.optimization_barrier((near_core, far_side, far_cross, wo_core))
    near_core = lax.ppermute(near_core, "core", swap)
    wo_parts = [wo, wo_core, wo_side]
    return pl.pallas_call(
        functools.partial(out_kernel, planes),
        out_shape=jax.ShapeDtypeStruct((rows, width), BF16),
        in_specs=[pl.BlockSpec(memory_space=pltpu.SMEM)] + [vm] * 7,
        out_specs=vm,
        scratch_shapes=[pltpu.VMEM((width, width), BF16)],
        compiler_params=limit,
        cost_estimate=work(3),
        name="mixed",
    )(jnp.stack([me, plane]).astype(I32), near, near_core, far_side, far_cross, *wo_parts)


def solution(mesh):
    groups, ctx = mesh.shape["groups"], mesh.shape["ctx"]
    planes = ctx // 4
    mesh4 = Mesh(mesh.devices.reshape(groups, planes, 2, 2), ("groups", "plane", "side", "core"))
    toks = ("groups", "plane", "side", "core")
    par = ("plane", "side", "core")
    in_specs = (P(toks, None), P(par, None), P(par, None), P(), P(toks), P(toks), P(toks))
    return jax.shard_map(
        functools.partial(local, groups, planes), mesh=mesh4, in_specs=in_specs, out_specs=P(toks, None), check_vma=False
    )
```

```python
import functools
import math

import jax
import jax.numpy as jnp
from jax import lax
from jax.experimental import pallas as pl
from jax.experimental.pallas import tpu as pltpu
from jax.sharding import Mesh, PartitionSpec as P

BIG = 2.0**100
TIMES = 104
SEG_BITS = 8
TILE = 256
ID_ROWS = 16
LOG2E = math.log2(math.e)
F32 = jnp.float32
BF16 = jnp.bfloat16
I32 = jnp.int32


def pick_kernel(width, cols, wide, pairs, who_ref, w_ref, *outs):
    me, half = who_ref[0], who_ref[1]
    for step, out in enumerate(outs):
        to = me ^ step
        for a in range(3):
            for b in range(pairs):
                at = pl.multiple_of(a * width + to * cols + (half ^ b if pairs == 1 else b) * wide, wide)
                out[:, (a * pairs + b) * wide : (a * pairs + b + 1) * wide] = w_ref[:, pl.ds(at, wide)]


def project_kernel(cols, plan, queries, planes, couple, who_ref, *refs):
    n = len(plan)
    k_ref, vt_ref, qt_ref, w = refs[-4:]
    xs, parts = refs[:n], refs[n:-4]
    me, plane, half = who_ref[0], who_ref[1], who_ref[2]
    wide = cols // 2
    rows = w.shape[0] // (4 * planes)
    for i, part in enumerate(parts):
        pair = half if i == 0 else 1 - half
        for p in range(planes):
            source = lax.rem(plane + planes - p, planes)
            for step in range(4):
                to = pl.multiple_of((4 * source + (me ^ step)) * rows, rows)
                block = part[(4 * p + step) * rows : (4 * p + step + 1) * rows, :]
                if couple:
                    for a in range(3):
                        at = pl.multiple_of(a * cols + pair * wide, wide)
                        w[pl.ds(to, rows), pl.ds(at, wide)] = block[:, a * wide : (a + 1) * wide]
                else:
                    w[pl.ds(to, rows), :] = block
    for x, (at, rows) in zip(xs, plan):
        out = jnp.dot(x[0:rows, :], w[:, cols:], preferred_element_type=F32)
        k_ref[at : at + rows, :] = out[:, :cols].astype(BF16)
        vt_ref[:, at : at + rows] = out[:, cols:].astype(BF16).T
        if at in queries:
            out = jnp.dot(x[0:rows, :], w[:, :cols], preferred_element_type=F32)
            q = (out.astype(BF16) * 0.125).astype(BF16)
            qt_ref[:, queries[at] : queries[at] + rows] = q.T


def mask_kernel(keys_ref, asks_ref, fk_ref, vk_ref, fqt_ref):
    bit0, bit1, last = TIMES, TIMES + SEG_BITS, TIMES + 2 * SEG_BITS

    def bit(seg, row, start):
        return (seg >> jnp.clip(row - start, 0, 30)) & 1

    for at in range(0, keys_ref.shape[1], 2 * TILE):
        n = 2 * TILE
        seg, var, time, gone = (keys_ref[i : i + 1, at : at + n] for i in range(4))
        row = lax.broadcasted_iota(I32, (128, n), 0)
        late = jnp.where(time > row, 1, 0)
        outside = jnp.where(row == last, gone, 0)
        off = jnp.where(row < bit0, late, jnp.where(row < bit1, bit(seg, row, bit0), 0))
        off = jnp.where((row >= bit1) & (row < last), 1 - bit(seg, row, bit1), off) + outside
        fk_ref[at : at + n, :] = (off.astype(F32) * -BIG).T.astype(BF16)
        vk_ref[at : at + n, :] = jnp.broadcast_to(var, (128, n)).T
    for at in range(0, asks_ref.shape[1], 2 * TILE):
        n = 2 * TILE
        seg, time = asks_ref[0:1, at : at + n], asks_ref[1:2, at : at + n]
        row = lax.broadcasted_iota(I32, (128, n), 0)
        on = jnp.where(row < bit0, jnp.where(time == row, 1, 0), jnp.where(row < bit1, 1 - bit(seg, row, bit0), 0))
        on = jnp.where((row >= bit1) & (row < last), bit(seg, row, bit1), on) + jnp.where(row == last, 1, 0)
        fqt_ref[:, at : at + n] = on.astype(F32).astype(BF16)


def attend_kernel(
    hsize, q0, nq, tab_ref, delta_ref, k_ref, vt_ref, qt_ref, fk_ref, fqt_ref, vk_ref, vq_ref, o_ref, qa0, qa1, sc0, sc1, m0, m1
):
    qi = pl.program_id(0)
    qas, scs, ms = (qa0, qa1), (sc0, sc1), (m0, m1)
    nt = sc0.shape[0]
    wide = nt + 1
    two = 2 * hsize

    def place(q, kk):
        return pl.multiple_of(tab_ref[(q0 + q) * wide + kk], TILE)

    def lanes(q):
        return pl.ds(pl.multiple_of((q0 + q) * TILE, TILE), TILE)

    def prep():
        zero = jnp.zeros((hsize, TILE), BF16)
        for j, qa in enumerate(qas):
            qa[0:hsize, 0:TILE] = qt_ref[two * j : two * j + hsize, lanes(qi)]
            qa[0:hsize, TILE:] = zero
            qa[hsize:two, 0:TILE] = zero
            qa[hsize:two, TILE:] = qt_ref[two * j + hsize : two * (j + 1), lanes(qi)]
            f = fqt_ref[:, lanes(qi)]
            qa[two:, 0:TILE] = f
            qa[two:, TILE:] = f

    def scores(j, kk, share, m):
        at = place(qi, kk)
        lhs = jnp.concatenate([k_ref[pl.ds(at, TILE), two * j : two * (j + 1)], fk_ref[pl.ds(at, TILE), :]], axis=1)
        s = jnp.dot(lhs, qas[j][...], preferred_element_type=F32)
        if kk in (0, nt - 1):
            r = lax.broadcasted_iota(I32, (TILE, TILE), 0)
            p = lax.broadcasted_iota(I32, (TILE, TILE), 1)
            ok = (r > p) if kk == 0 else (r < p)
            s = jnp.where(jnp.concatenate([ok, ok], axis=1), s, -BIG)
        if share:
            vk = vk_ref[pl.ds(at, TILE), :]
            same = jnp.concatenate([vk, vk], axis=1) == vq_ref[:, lanes(qi)]
            s = s + jnp.concatenate(
                [jnp.where(same, delta_ref[2 * j], 0.0), jnp.where(same, delta_ref[2 * j + 1], 0.0)], axis=1
            )
        scs[j][kk] = s
        return jnp.maximum(m, jnp.max(s.reshape(TILE // 8, 8, 2 * TILE), axis=0))

    def mix(j, q, kk, top, state):
        tot, oa, ob = state
        vt = vt_ref[two * j : two * (j + 1), pl.ds(place(q, kk), TILE)]
        w = jnp.exp2((scs[j][kk] - top) * LOG2E)
        tot = tot + jnp.sum(w.reshape(TILE // 8, 8, 2 * TILE), axis=0)
        wb = w.astype(BF16)
        oa = oa + jnp.dot(vt[:hsize], wb[:, :TILE], preferred_element_type=F32)
        ob = ob + jnp.dot(vt[hsize:], wb[:, TILE:], preferred_element_type=F32)
        return tot, oa, ob

    def phase(j, old, q, share):
        m = jnp.full((8, 2 * TILE), -BIG, F32)
        z = jnp.zeros((hsize, TILE), F32)
        state = (jnp.zeros((8, 2 * TILE), F32), z, z)
        if old is not None:
            top = jnp.max(ms[old][...], axis=0, keepdims=True)
        for kk in range(nt):
            if j is not None:
                m = scores(j, kk, share or abs(kk - nt // 2) <= 1, m)
            if old is not None:
                state = mix(old, q, kk, top, state)
        if j is not None:
            ms[j][...] = m
        if old is not None:
            tot, oa, ob = state
            tot = jnp.sum(tot, axis=0, keepdims=True)
            o = jnp.concatenate([oa / tot[:, :TILE], ob / tot[:, TILE:]], axis=0)
            o_ref[pl.ds(pl.multiple_of(q * TILE, TILE), TILE), two * old : two * (old + 1)] = o.T.astype(BF16)

    prep()
    far = tab_ref[(q0 + qi) * wide + nt]
    for share in (False, True):

        @pl.when((far != 0) == share)
        def _(share=share):
            @pl.when(qi == 0)
            def _():
                phase(0, None, 0, share)

            @pl.when(qi > 0)
            def _():
                phase(0, 1, qi - 1, share)

            phase(1, 0, qi, share)

    @pl.when(qi == nq - 1)
    def _():
        phase(None, 1, qi, False)


def out_kernel(planes, who_ref, a0, a1, a2, a3, w0, w1, w2, o_ref, w):
    me, plane = who_ref[0], who_ref[1]
    for part, place in ((w0, me), (w1.at[0], me ^ 1), (w2, me ^ 2), (w1.at[1], me ^ 3)):
        rows = part.shape[0] // planes
        for i in range(planes):
            source = lax.rem(plane + planes - i, planes)
            at = pl.multiple_of((4 * source + place) * rows, rows)
            w[pl.ds(at, rows), :] = part[i * rows : (i + 1) * rows, :]
    total = None
    for a, place in ((a0, me), (a1, me ^ 1), (a2, me ^ 2), (a3, me ^ 3)):
        cols = a.shape[1]
        part = jnp.dot(a[...], w[pl.ds(pl.multiple_of(place * cols, cols), cols), :], preferred_element_type=F32)
        total = part if total is None else total + part
    o_ref[...] = total.astype(BF16)


def in_plane(blocks):
    swap = [(0, 1), (1, 0)]
    cross = [(0, 3), (1, 2), (2, 1), (3, 0)]
    return [
        lax.ppermute(blocks[0], "core", swap),
        lax.ppermute(blocks[1], "side", swap),
        lax.ppermute(blocks[2], ("side", "core"), cross),
    ]


def work(micros):
    return pl.CostEstimate(flops=int(micros * 1.1e9), transcendentals=0, bytes_accessed=1 << 20)


def turns(block, planes):
    return [block] + [
        lax.ppermute(block, "plane", [(i, (i + s) % planes) for i in range(planes)]) for s in range(1, planes)
    ]


def local(groups, planes, tokens, w_qkv, w_out, var_bias, seg_id, var_id, time_id):
    rows, width = tokens.shape
    heads = var_bias.shape[1]
    hsize = width // heads
    cols = width // 4
    core = lax.axis_index("core")
    side = lax.axis_index("side")
    plane = lax.axis_index("plane")
    swap = [(0, 1), (1, 0)]
    cross = [(0, 3), (1, 2), (2, 1), (3, 0)]
    pair = ("plane", "side")
    native, passed, direct = [], [], []
    for p in range(planes - 1):
        native += [(2 * (p + 1), 2 * p), (2 * p + 1, 2 * (p + 1) + 1)]
        passed += [(2 * p, 2 * (p + 1)), (2 * (p + 1) + 1, 2 * p + 1)]
        direct += [(2 * p + 1, 2 * (p + 1)), (2 * (p + 1), 2 * p + 1)]

    group = lax.axis_index("groups")
    me = 2 * side + core
    wide = cols // 2
    mate = [(g, g ^ 1) for g in range(groups)]
    couple = groups % 2 == 0
    picked = pl.pallas_call(
        functools.partial(pick_kernel, width, cols, wide, 1 if couple else 2),
        out_shape=[jax.ShapeDtypeStruct((w_qkv.shape[0], (3 if couple else 6) * wide), BF16)] * 4,
        in_specs=[pl.BlockSpec(memory_space=pltpu.SMEM), pl.BlockSpec(memory_space=pltpu.VMEM)],
        out_specs=[pl.BlockSpec(memory_space=pltpu.VMEM)] * 4,
        cost_estimate=work(1),
        name="pick",
    )(jnp.stack([me, group % 2]).astype(I32), w_qkv)
    came = in_plane(picked[1:])
    plane_w = jnp.concatenate([picked[0]] + came, 0)
    w_parts = turns(plane_w, planes)
    turned = w_parts[1:]
    half_w = jnp.concatenate(w_parts, 0)
    if couple:
        w_parts = [half_w, lax.ppermute(half_w, "groups", mate)]
    else:
        w_parts = [half_w]

    cut = rows // 2
    tokens = lax.optimization_barrier((tokens, picked))[0]
    digits = jnp.stack([seg_id, var_id >> 4, var_id & 15, time_id], 0).astype(BF16).reshape(4 * rows // width, width)
    digits = jnp.pad(digits, ((0, ID_ROWS - digits.shape[0]), (0, 0)))
    first = jnp.concatenate([tokens[:cut], digits], 0)
    whole = jnp.concatenate([tokens, digits], 0)
    wo = turns(lax.optimization_barrier((w_out, picked))[0], planes)
    first, second, _, wo = lax.optimization_barrier((first, tokens[cut:], came, wo))
    other = [lax.ppermute(x, "side", swap) for x in (first, second)]
    first_z = lax.optimization_barrier((first, turned))[0]
    mine = [lax.ppermute(first_z, pair, native)]
    theirs = [lax.ppermute(other[0], pair, passed)]
    whole, second, passing, _, _ = lax.optimization_barrier(
        (whole, second, other[1], (mine[0], theirs[0]), w_parts)
    )
    mine.append(lax.ppermute(second, pair, native))
    theirs.append(lax.ppermute(passing, pair, passed))
    other[1] = passing
    peers = [lax.ppermute(x, "core", swap) for x in (whole, other[0], mine[0], theirs[0])]

    def ids_of(x, n):
        return x[n : n + 4 * rows // width].reshape(4, rows).astype(I32)

    ids = [ids_of(x, cut) for x in (other[0], mine[0], theirs[0])]
    ids += [ids_of(peers[0], rows)] + [ids_of(x, cut) for x in peers[1:]]
    seg, hi, lo, time = jnp.concatenate([ids_of(digits, 0)] + ids, 1)
    var = hi * 16 + lo

    nk = 8 * rows
    per = rows // TILE
    nt = 4 * per + 1
    nq = 2 * per
    below = jnp.where(side == 0, 3, 2)
    stream = jnp.arange(4, dtype=I32)
    there = jnp.where(stream == below, plane > 0, jnp.where(stream == 5 - below, plane < planes - 1, True))
    there = jnp.tile(there, 2)
    gone = jnp.repeat(~there, rows).astype(I32)

    def asked(a):
        return jnp.concatenate([a[0:rows], a[4 * rows : 5 * rows], a[rows : 2 * rows], a[5 * rows : 6 * rows]], 0)

    var_q = asked(var)
    keys_ids = jnp.stack([seg, var, time, gone], 0)
    vm = pl.BlockSpec(memory_space=pltpu.VMEM)
    fk, vk, fqt = pl.pallas_call(
        mask_kernel,
        out_shape=[
            jax.ShapeDtypeStruct((nk, 128), BF16),
            jax.ShapeDtypeStruct((nk, 128), I32),
            jax.ShapeDtypeStruct((128, 4 * rows), BF16),
        ],
        in_specs=[vm] * 2,
        out_specs=[vm] * 3,
        cost_estimate=work(2),
        name="masks",
    )(keys_ids, jnp.stack([asked(seg), asked(time)], 0))

    qtile = jnp.arange(4 * per, dtype=I32)
    qblock = qtile // per
    q_side = jnp.where(qblock // 2 == 0, side, 1 - side)
    q_core = jnp.where(qblock % 2 == 0, core, 1 - core)
    q_win = (2 + 2 * q_side + q_core) * per + qtile % per
    k_win = q_win[:, None] - 2 * per + jnp.arange(nt, dtype=I32)[None, :]
    k_block = k_win // per
    k_token = k_block // 2
    k_stream = jnp.where(
        side == 0,
        jnp.where(k_token == 0, 3, k_token - 1),
        jnp.where(k_token == 3, 3, 2 - k_token),
    )
    k_place = (jnp.where(k_block % 2 == core, 0, 4) + k_stream) * per + k_win % per
    code = (seg * 1024 + var).reshape(nk // TILE, TILE)
    lo, hi = code.min(1), code.max(1)
    tile = jnp.arange(8 * per, dtype=I32)
    t_block = tile // per
    t_core = jnp.where(t_block // 4 == 0, core, 1 - core)
    t_stream = t_block % 4
    t_token = jnp.where(side == 0, (t_stream + 1) % 4, jnp.where(t_stream == 3, 3, 2 - t_stream))
    apart = ((2 * t_token + t_core) * per + tile % per)[None, :] - q_win[:, None]
    apart = jnp.abs(apart)
    hi_q = jnp.concatenate([hi[b * per : (b + 1) * per] for b in (0, 4, 1, 5)])
    lo_q = jnp.concatenate([lo[b * per : (b + 1) * per] for b in (0, 4, 1, 5)])
    share = (lo[None, :] <= hi_q[:, None]) & (hi[None, :] >= lo_q[:, None])
    share = share & jnp.repeat(there, per)[None, :] & (apart > 1) & (apart <= nt // 2)
    table = jnp.concatenate([k_place * TILE, share.any(1, keepdims=True).astype(I32)], 1).reshape(-1)
    delta = lax.dynamic_slice_in_dim(var_bias[0] - var_bias[1], (2 * side + core) * (heads // 4), heads // 4, 0)

    who = jnp.stack([me, plane, group % 2]).astype(I32)
    masks = (fk, fqt, vk, table)
    rest = [lax.ppermute(passing, "core", swap)]
    lasts, masks = lax.optimization_barrier(((mine[1], theirs[1]), masks))
    fk, fqt, vk, table = masks
    rest += [lax.ppermute(x, "core", swap) for x in lasts]
    held = [(0, rows, tokens), (4 * rows, rows, peers[0])]
    for i, (one, two) in enumerate((other, (mine[0], lasts[0]), (theirs[0], lasts[1]))):
        held += [((i + 1) * rows, cut, one), ((i + 1) * rows + cut, cut, two)]
        held += [((i + 5) * rows, cut, peers[i + 1]), ((i + 5) * rows + cut, cut, rest[i])]
    plan = tuple((at, n) for at, n, _ in held)
    xs = [x for _, _, x in held]
    limit = pltpu.CompilerParams(vmem_limit_bytes=24 << 20)
    queries = {}
    for at, _ in plan:
        block = at // rows
        if block in (0, 1, 4, 5):
            queries[at] = {0: 0, 4: rows, 1: 2 * rows, 5: 3 * rows}[block] + at % rows
    k, vt, qt = pl.pallas_call(
        functools.partial(project_kernel, cols, plan, queries, planes, couple),
        out_shape=[
            jax.ShapeDtypeStruct((nk, cols), BF16),
            jax.ShapeDtypeStruct((cols, nk), BF16),
            jax.ShapeDtypeStruct((cols, 4 * rows), BF16),
        ],
        in_specs=[pl.BlockSpec(memory_space=pltpu.SMEM)] + [vm] * (len(xs) + len(w_parts)),
        out_specs=[vm] * 3,
        scratch_shapes=[pltpu.VMEM((width, 3 * cols), BF16)],
        compiler_params=limit,
        cost_estimate=work(12),
        name="project",
    )(who, *xs, *w_parts)

    wo, k, vt, qt = lax.optimization_barrier((jnp.concatenate(wo, 0), k, vt, qt))
    wo_side = lax.ppermute(wo, "side", swap)

    def attend(q0):
        return pl.pallas_call(
            functools.partial(attend_kernel, hsize, q0, nq),
            out_shape=jax.ShapeDtypeStruct((2 * rows, cols), BF16),
            grid_spec=pltpu.PrefetchScalarGridSpec(
                num_scalar_prefetch=2,
                grid=(nq,),
                in_specs=[vm] * 7,
                out_specs=vm,
                scratch_shapes=[pltpu.VMEM((2 * hsize + 128, 2 * TILE), BF16)] * 2
                + [pltpu.VMEM((nt, TILE, 2 * TILE), F32)] * 2
                + [pltpu.VMEM((8, 2 * TILE), F32)] * 2,
            ),
            compiler_params=limit,
            cost_estimate=work(16),
            name="attend",
        )(table, delta, k, vt, qt, fk, fqt, vk, var_q[None, :])

    far = attend(nq)
    far_side, far_cross, wo_side = lax.optimization_barrier((far[:rows], far[rows:], wo_side))
    far_side = lax.ppermute(far_side, "side", swap)
    far_cross = lax.ppermute(far_cross, ("side", "core"), cross)
    wo_core = lax.ppermute(jnp.stack([wo, wo_side]), "core", swap)
    near = attend(0)
    near_core, near = near[rows:], near[:rows]
    near_core, far_side, far_cross, wo_core = lax.optimization_barrier((near_core, far_side, far_cross, wo_core))
    near_core = lax.ppermute(near_core, "core", swap)
    wo_parts = [wo, wo_core, wo_side]
    return pl.pallas_call(
        functools.partial(out_kernel, planes),
        out_shape=jax.ShapeDtypeStruct((rows, width), BF16),
        in_specs=[pl.BlockSpec(memory_space=pltpu.SMEM)] + [vm] * 7,
        out_specs=vm,
        scratch_shapes=[pltpu.VMEM((width, width), BF16)],
        compiler_params=limit,
        cost_estimate=work(3),
        name="mixed",
    )(jnp.stack([me, plane]).astype(I32), near, near_core, far_side, far_cross, *wo_parts)


def solution(mesh):
    groups, ctx = mesh.shape["groups"], mesh.shape["ctx"]
    planes = ctx // 4
    mesh4 = Mesh(mesh.devices.reshape(groups, planes, 2, 2), ("groups", "plane", "side", "core"))
    toks = ("groups", "plane", "side", "core")
    par = ("plane", "side", "core")
    in_specs = (P(toks, None), P(par, None), P(par, None), P(), P(toks), P(toks), P(toks))
    return jax.shard_map(
        functools.partial(local, groups, planes), mesh=mesh4, in_specs=in_specs, out_specs=P(toks, None), check_vma=False
    )
```
